512 devices in a mesh: space: 16 (over y, x_lo, core), tm: 32 (over x_hi, z).
Axes of the slice: x: 4 (x_hi: 2, x_lo: 2; x = x_hi * 2 + x_lo), y: 4, z: 16, core: 2. Of those that a mesh axis runs over, the one named last changes fastest.
Arguments:
- eigenvectors: bfloat16 [32, 2, 3, 16, 256, 256], P('tm', None, None, 'space'), may hold values from -0.0390625 to 0.0390625
- momenta: int32 [6, 3], replicated, may hold values from -2 to 2
- displacement: int32 [6], replicated, may hold values from 0 to 3, as said below
- source_times: int32 [4], replicated, may hold values from 0 to 31
- perambulators: bfloat16 [32, 4, 2, 256, 256], P('tm', None, None, 'space'), may hold values from -2 to 2
Outputs:
- correlator: float32 [32, 4, 2, 6, 6], P('tm')
- two_meson: float32 [32, 4, 2, 6, 6], P('tm')
The draws below stay inside these ranges and needn't reach their ends.
Inputs may be any that keep to these rules, and one draw needn't show every extreme that they name: `displacement`: 0 keeps the site, 1, 2, 3 move one site forward along x, y, z; each of the four values is used by some operator.
All inputs are finite; a program needn't handle non-finite values.
Results may differ from the reference program's by a relative error of at most 0.0078.
Values may be sent and summed in bfloat16 or wider, within the bound.
A program may use at most 64 MiB of HBM per device.

```python
import math
import jax
import jax.numpy as jnp
from jax import lax

NVEC = 256
OPS = 6
LX = 16
LY = 16
NSRC = 4
NZ = 16
NT = 32


def draw_displacement(key, part):
    leading = jax.random.permutation(jax.random.fold_in(key, 11), 4).astype(jnp.int32)
    remaining = jax.random.randint(jax.random.fold_in(key, 12), (OPS - 4,), 0, 4, dtype=jnp.int32)
    shuffle = jax.random.permutation(jax.random.fold_in(key, 13), OPS)
    return jnp.concatenate([leading, remaining])[shuffle].astype(jnp.int32)


def place_ends(array, stream_key, low, largest):
    place = [jax.random.randint(jax.random.fold_in(stream_key, axis), (), 0, length) for axis, length in enumerate(array.shape)]
    widest = array.shape.index(max(array.shape))
    neighbour = place[:widest] + [(place[widest] + 1) % array.shape[widest]] + place[widest + 1:]
    return array.at[tuple(place)].set(low).at[tuple(neighbour)].set(largest)


def levels(own_key, extent, shards, least, high):
    def one(axis_at, blocks):
        draws = jax.random.uniform(jax.random.fold_in(jax.random.fold_in(own_key, 6), axis_at), (blocks,), jnp.float32, least / len(shards), high / len(shards))
        return jnp.repeat(jnp.exp(draws), extent[axis_at] // blocks).reshape((-1,) + (1,) * (len(extent) - axis_at - 1))

    gain = one(*shards[0])
    for cut in shards[1:]:
        gain = gain * one(*cut)
    return gain


def centred(stream_key, dims, spread, most, cuts=(), kind=jnp.bfloat16):
    entries = spread * jax.random.normal(stream_key, dims, jnp.float32)
    if cuts:
        entries = entries * levels(stream_key, dims, cuts, -0.22, 0.18)
    return jnp.clip(entries, -most, most).astype(kind)


def setup_inputs(seed: int = 0) -> dict:
    splits = jax.random.split(jax.random.key(seed), 6)
    return {
        "eigenvectors": centred(splits[0], (NT, 2, 3, NZ, LY * LX, NVEC), (6 * LX * LY * NZ) ** -0.5, 0.0390625, ((0, 32), (3, 16))),
        "momenta": place_ends(jax.random.randint(splits[1], (OPS, 3), -2, 3), jax.random.fold_in(splits[1], 1), -2, 2).astype(jnp.int32),
        "displacement": draw_displacement(jax.random.fold_in(splits[5], 71), 0),
        "source_times": place_ends(jax.random.randint(splits[3], (NSRC,), 0, NT), jax.random.fold_in(splits[3], 1), 0, NT - 1).astype(jnp.int32),
        "perambulators": centred(splits[4], (NT, NSRC, 2, NVEC, NVEC), (max(1, 2 * NVEC * NVEC // (3 * LX * LY * NZ))) ** -0.5, 2.0, ((0, 32), (3, 16))),
    }


def contract(formula, left, right):
    return jnp.einsum(formula, left.astype(jnp.float32), right.astype(jnp.float32), precision=lax.Precision.HIGHEST, preferred_element_type=jnp.float32)


def complex_product(formula, left, right, conjugate):
    if conjugate:
        real_part = contract(formula, left[0], right[0]) + contract(formula, left[1], right[1])
        imaginary_part = contract(formula, left[1], right[0]) - contract(formula, left[0], right[1])
    else:
        real_part = contract(formula, left[0], right[0]) - contract(formula, left[1], right[1])
        imaginary_part = contract(formula, left[0], right[1]) + contract(formula, left[1], right[0])
    return real_part, imaginary_part


def plane_angles(momenta, operator, z_coords, z_extent):
    plane = jnp.arange(LY * LX, dtype=jnp.int32)
    along_x = ((momenta[operator, 0] * (plane % LX)) % LX).astype(jnp.float32) * (2.0 * math.pi / LX)
    along_y = ((momenta[operator, 1] * (plane // LX)) % LY).astype(jnp.float32) * (2.0 * math.pi / LY)
    along_z = ((momenta[operator, 2] * z_coords) % z_extent).astype(jnp.float32) * (2.0 * math.pi / z_extent)
    return (along_x + along_y)[None, :] + along_z[:, None]


def shift_first(field):
    layout = field.shape
    opened = field.reshape(layout[:-2] + (LY, LX, layout[-1]))
    return jnp.roll(opened, -1, axis=-2).reshape(layout)


def shift_second(field):
    layout = field.shape
    opened = field.reshape(layout[:-2] + (LY, LX, layout[-1]))
    return jnp.roll(opened, -1, axis=-3).reshape(layout)


def shift_third(field):
    return jnp.roll(field, -1, axis=-3)


def unmoved(field):
    return field


def weighted(real_in, imaginary_in, angles):
    cosine = jnp.cos(angles)[:, :, None]
    sine = jnp.sin(angles)[:, :, None]
    real_wide = real_in.astype(jnp.float32)
    imaginary_wide = imaginary_in.astype(jnp.float32)
    w_real = (cosine * real_wide + sine * imaginary_wide).astype(jnp.bfloat16)
    w_imaginary = (cosine * imaginary_wide - sine * real_wide).astype(jnp.bfloat16)
    return w_real, w_imaginary


def reference(eigenvectors, momenta, displacement, source_times, perambulators):
    z_coords = jnp.arange(NZ, dtype=jnp.int32)

    def time_elementals(field):
        results = []
        for operator in range(OPS):
            shifted = lax.switch(displacement[operator], [unmoved, shift_first, shift_second, shift_third], field)
            angles = plane_angles(momenta, operator, z_coords, NZ)
            w_real, w_imaginary = weighted(shifted[0], shifted[1], angles)
            pair = complex_product('kn,kc->cn', (w_real.reshape(-1, NVEC), w_imaginary.reshape(-1, NVEC)), (field[0].reshape(-1, NVEC), field[1].reshape(-1, NVEC)), True)
            results.append(jnp.stack(pair))
        return jnp.stack(results)

    elements = lax.map(time_elementals, eigenvectors).astype(jnp.bfloat16)

    def time_traces(inputs):
        sink, peram_slice = inputs
        collected = []
        for source in range(NSRC):
            source_block = lax.dynamic_index_in_dim(elements, source_times[source].astype(jnp.int32), 0, keepdims=False)
            peram_pair = (peram_slice[source, 0], peram_slice[source, 1])
            left = complex_product('aij,jk->aik', (sink[:, 0], sink[:, 1]), peram_pair, False)
            right = complex_product('bkl,il->bki', (source_block[:, 0], source_block[:, 1]), peram_pair, True)
            traces = complex_product('aik,bki->ab', left, right, False)
            collected.append(jnp.stack(traces))
        return jnp.stack(collected)

    correlator = lax.map(time_traces, (elements, perambulators))
    diagonal = jnp.diagonal(correlator, axis1=3, axis2=4)
    diag_real = diagonal[:, :, 0]
    diag_imaginary = diagonal[:, :, 1]
    pair_real = diag_real[:, :, :, None] * diag_real[:, :, None, :] - diag_imaginary[:, :, :, None] * diag_imaginary[:, :, None, :]
    pair_imaginary = diag_real[:, :, :, None] * diag_imaginary[:, :, None, :] + diag_imaginary[:, :, :, None] * diag_real[:, :, None, :]
    two_meson = jnp.stack([pair_real, pair_imaginary], axis=2)
    return correlator, two_meson
```

```python
import functools
import math

import jax
import jax.numpy as jnp
from jax import lax
from jax.experimental import pallas as pl
from jax.experimental.pallas import tpu as pltpu
from jax.sharding import PartitionSpec as P

MESH = pl.DeviceIdType.MESH
F32 = jnp.float32
BF16 = jnp.bfloat16
OPS = 6
SRC = 4
CHIPS = 8
NV = 256
ROWS = 16
COSINE = [math.cos(2.0 * math.pi * m / 16) for m in range(16)]
SINE = [math.sin(2.0 * math.pi * m / 16) for m in range(16)]


def nt(left, right, precision=None):
    return lax.dot_general(
        left, right, (((1,), (1,)), ((), ())), precision=precision, preferred_element_type=F32
    )


def fold(block):
    halves = block[:, :128] + block[:, 128:]
    return halves[:8] + halves[8:]


def kernel(
    ring, v_hbm, mom, disp, src, p_hbm, out_ref,
    sh3, zb, vt, rhs, ctb, part, prt, sb, rsr, et, xhb, cs, rsend, rrecv, pg, pct, lt, wb, es, red, res,
    perm, pos, dsort,
    loc_sem, zs_send, zs_recv, pr_send, pr_recv, rs_send, rs_recv, ag_send, ag_recv, fw_send, fw_recv,
    xh_send, xh_recv, bc_send, bc_recv, pgs, pgr, pfs, pfr, ps_send, ps_recv,
):
    space = 2 * CHIPS
    half = ring // 2
    hops = (half, ring - 1 - half)
    steps = tuple(OPS + h - 1 for h in hops)
    r = lax.axis_index("space")
    t = lax.axis_index("tm")
    chip = r // 2
    core = r % 2
    xh = t // ring
    z = t % ring
    partner = 2 * chip + 1 - core
    ahead = (xh * ring + (z + 1) % ring, xh * ring + (z + ring - 1) % ring)
    across = (1 - xh) * ring + z
    own = core * 128 + chip * ROWS

    def peer(d):
        return (chip + d) % CHIPS

    def remote(src_ref, dst_ref, send, recv, axis, index):
        return pltpu.make_async_remote_copy(
            src_ref=src_ref, dst_ref=dst_ref, send_sem=send, recv_sem=recv,
            device_id={axis: index}, device_id_type=MESH,
        )

    def mine(ref, i):
        return ref.at[i, pl.ds(pl.multiple_of(own, ROWS), ROWS)]

    def rows_of(q):
        return pl.ds(pl.multiple_of(core * 128 + q * ROWS, ROWS), ROWS)

    def side(c):
        return pl.ds(pl.multiple_of(c * 128, 128), 128)

    def z_copy():
        return remote(v_hbm, zb, zs_send, zs_recv, "space", (r + space - 1) % space)

    def pair_copy(i):
        return remote(part.at[i, side(1 - core)], prt.at[i], pr_send.at[i], pr_recv.at[i], "space", partner)

    def rs_copy(i, to, frm):
        return remote(sb.at[i, to], rsr.at[i, frm], rs_send.at[i], rs_recv.at[i, frm], "space", 2 * to + core)

    def ag_copy(i, to, frm):
        rows = rows_of(frm)
        return remote(et.at[i, rows], et.at[i, rows], ag_send.at[i], ag_recv.at[i, frm], "space", 2 * to + core)

    def fw_copy(i, c):
        return remote(et.at[i, side(c)], et.at[i, side(c)], fw_send.at[i], fw_recv.at[i], "space", partner)

    def xh_copy(i):
        return remote(mine(et, i), xhb.at[i], xh_send.at[i], xh_recv.at[i], "tm", across)

    def bc_copy(w, k, s, source):
        return remote(source, rrecv.at[w, k, s], bc_send.at[w, k], bc_recv.at[w, k, s], "tm", ahead[w])

    def pg_copy(to, frm):
        return remote(p_hbm, pg.at[frm, core], pgs, pgr.at[frm], "space", 2 * to + core)

    def pf_copy(c):
        return remote(pg.at[:, c], pg.at[:, c], pfs, pfr, "space", partner)

    def ps_copy(to, frm):
        return remote(res.at[frm], res.at[frm], ps_send, ps_recv.at[frm], "space", to)

    barrier = pltpu.get_barrier_semaphore()
    v_copy = pltpu.make_async_copy(v_hbm, sh3.at[0], loc_sem.at[0])
    v_copy.start()
    p_copy = pltpu.make_async_copy(p_hbm, pg.at[chip, core], loc_sem.at[1])
    p_copy.start()

    @pl.loop(1, space)
    def _(d):
        pl.semaphore_signal(barrier, inc=1, device_id={"space": (r + d) % space}, device_id_type=MESH)

    for other in (*ahead, across):
        pl.semaphore_signal(barrier, inc=1, device_id={"tm": other}, device_id_type=MESH)
    pl.semaphore_wait(barrier, space + 2)
    z_copy().start()

    place = []
    for o in range(OPS):
        before = jnp.int32(0)
        for q in range(OPS):
            if q != o:
                low = disp[q] <= disp[o] if q < o else disp[q] < disp[o]
                before = before + jnp.where(low, 1, 0)
        place.append(before)
        pos[o] = before
    for j in range(OPS):
        which = jnp.int32(0)
        for o in range(OPS):
            which = which + jnp.where(place[o] == j, o, 0)
        perm[j] = which
        dsort[j] = disp[which]

    site = lax.broadcasted_iota(jnp.int32, (128, NV), 1)
    line = lax.broadcasted_iota(jnp.int32, (128, NV), 0)
    turns = jnp.zeros((128, NV), jnp.int32)
    for j in range(OPS):
        o = perm[j]
        turns = jnp.where(line == j, mom[o, 0] * (site & 15) + mom[o, 1] * (site >> 4) + mom[o, 2] * r, turns)
    turns = turns & 15
    for a, table in enumerate((COSINE, SINE)):
        values = jnp.zeros((128, NV), F32)
        for m in range(16):
            values = jnp.where(turns == m, F32(table[m]), values)
        flipped = values.T
        for j in range(OPS):
            ctb[j, a] = jnp.broadcast_to(flipped[:, j : j + 1], (NV, 128))

    v_copy.wait()
    row = lax.broadcasted_iota(jnp.int32, (NV, NV), 0)
    wraps = (row & 15) == 15
    for p in range(6):
        wide = sh3[0, p].astype(F32)
        vt[:, p * NV : (p + 1) * NV] = wide.T.astype(BF16)
        sh3[1, p] = jnp.where(wraps, pltpu.roll(wide, 15, 0), pltpu.roll(wide, NV - 1, 0)).astype(BF16)
        sh3[2, p, : NV - 16] = sh3[0, p, 16:]
        sh3[2, p, NV - 16 :] = sh3[0, p, :16]

    def weigh(i, beyond):
        d = dsort[i]
        kept = jnp.minimum(d, 2)

        @pl.loop(0, 12)
        def _(step):
            color = step // 4
            top = pl.multiple_of((step % 4) * 64, 64)
            rows = pl.ds(top, 64)
            re = sh3[kept, color, rows]
            im = sh3[kept, 3 + color, rows]
            re = re.astype(F32)
            im = im.astype(F32)
            if beyond:
                moved = jnp.full((64, NV), d, jnp.int32) == 3
                re = jnp.where(moved, zb[color, rows].astype(F32), re)
                im = jnp.where(moved, zb[3 + color, rows].astype(F32), im)
            cosine = ctb[i, 0, rows]
            sine = ctb[i, 1, rows]
            cosine = jnp.concatenate([cosine, cosine], axis=1)
            sine = jnp.concatenate([sine, sine], axis=1)
            w_re = (cosine * re + sine * im).astype(BF16)
            w_im = (cosine * im - sine * re).astype(BF16)
            upper = pl.ds(pl.multiple_of(color * NV + top, 64), 64)
            lower = pl.ds(pl.multiple_of(3 * NV + color * NV + top, 64), 64)
            rhs[upper, :NV] = w_re
            rhs[upper, NV:] = w_im
            rhs[lower, :NV] = w_im
            rhs[lower, NV:] = -w_re

    def spread(k):
        here = et[k, pl.ds(pl.multiple_of(own, ROWS), ROWS)].astype(F32)
        there = xhb[k].astype(F32)
        for s in range(SRC):
            when = jnp.full((ROWS, 2 * NV), src[s], jnp.int32)
            value = jnp.where(when == t, here, there).astype(BF16)
            cs[s, k] = value

            for w in range(2):

                @pl.when(k == 0)
                def _():
                    rsend[w, k, s] = cs[s, k]

                @pl.when(k > 0)
                def _():
                    bc_copy(w, k - 1, s, rsend.at[w, k, s]).wait_recv()
                    come = rrecv[w, k - 1, s].astype(F32)
                    given = cs[s, k].astype(F32)
                    rsend[w, k, s] = jnp.where(when % ring == z, given, come).astype(BF16)

                bc_copy(w, k, s, rsend.at[w, k, s]).start()

    def relay(k):
        for s in range(SRC):
            for w in range(2):

                @pl.when(k < steps[w])
                def _():
                    bc_copy(w, k - 1, s, rrecv.at[w, k - 1, s]).wait_recv()
                    bc_copy(w, k, s, rrecv.at[w, k - 1, s]).start()

    @pl.loop(0, OPS + 4)
    def _(i):
        @pl.when(i < 3)
        def _():
            weigh(i, False)

        @pl.when(i == 3)
        def _():
            z_copy().wait_recv()

        @pl.when((i >= 3) & (i < OPS))
        def _():
            weigh(i, True)

        @pl.when(i < OPS)
        def _():
            part[i] = jnp.dot(vt[...], rhs[...], preferred_element_type=F32)
            pair_copy(i).start()

        @pl.when((i >= 1) & (i < OPS + 1))
        def _():
            k = i - 1
            pair_copy(k).wait_recv()
            sb[k] = (part[k, side(core)] + prt[k]).astype(BF16).reshape(CHIPS, ROWS, 2 * NV)

            @pl.loop(1, CHIPS)
            def _(d):
                rs_copy(k, peer(d), chip).start()

        @pl.when((i >= 2) & (i < OPS + 2))
        def _():
            k = i - 2
            total = part[k, pl.ds(pl.multiple_of(own, ROWS), ROWS)] + prt[k, pl.ds(pl.multiple_of(chip * ROWS, ROWS), ROWS)]
            for d in range(1, CHIPS):
                rs_copy(k, chip, peer(d)).wait_recv()
                total = total + rsr[k, peer(d)].astype(F32)
            et[k, pl.ds(pl.multiple_of(own, ROWS), ROWS)] = total.astype(BF16)
            xh_copy(k).start()

            @pl.loop(1, CHIPS)
            def _(d):
                ag_copy(k, peer(d), chip).start()

        @pl.when((i >= 3) & (i < OPS + 3))
        def _():
            k = i - 3
            xh_copy(k).wait_recv()
            spread(k)

        @pl.when(i >= 4)
        def _():
            k = i - 4

            @pl.loop(1, CHIPS)
            def _(d):
                ag_copy(k, chip, peer(d)).wait_recv()

            fw_copy(k, core).start()

        @pl.when(i == OPS)
        def _():
            @pl.loop(1, CHIPS)
            def _(d):
                pg_copy(peer(d), chip).start()

    relay(OPS)
    p_copy.wait()

    @pl.loop(1, CHIPS)
    def _(d):
        pg_copy(chip, peer(d)).wait_recv()

    pf_copy(core).start()
    relay(OPS + 1)
    pf_copy(1 - core).wait_recv()

    pick = lax.broadcasted_iota(jnp.int32, (ROWS, NV), 0) + own == lax.broadcasted_iota(jnp.int32, (ROWS, NV), 1)
    pick = jnp.where(pick, F32(1), F32(0)).astype(BF16)
    for s in range(SRC):
        for a in range(2):
            block = pg[:, :, s, a].reshape(NV, NV)
            pct[a * 64 + s * ROWS : a * 64 + (s + 1) * ROWS] = nt(pick, block).astype(BF16)

    @pl.loop(0, OPS)
    def _(a):
        @pl.when(a + OPS + 2 < max(steps))
        def _():
            relay(a + OPS + 2)

        fw_copy(a, 1 - core).wait_recv()
        u = nt(pct[...], et[a, :, :NV])
        v = nt(pct[...], et[a, :, NV:])
        lt[a, 0] = (u[:64] - v[64:]).reshape(SRC, ROWS, NV)
        lt[a, 1] = (v[:64] + u[64:]).reshape(SRC, ROWS, NV)

    for w in range(2):
        for s in range(SRC):
            bc_copy(w, steps[w] - 1, s, rsend.at[w, 0, s]).wait_recv()

    red[...] = jnp.zeros_like(red)

    @pl.loop(0, SRC)
    def _(s):
        dist = (z - src[s]) & (ring - 1)
        near = jnp.full((ROWS, 2 * NV), dist, jnp.int32)

        @pl.loop(0, OPS)
        def _(o):
            up = jnp.minimum(jnp.maximum(o + dist - 1, 0), steps[0] - 1)
            down = jnp.minimum(jnp.maximum(o + ring - 1 - dist, 0), steps[1] - 1)
            value = jnp.where(near <= half, rrecv[0, up, s].astype(F32), rrecv[1, down, s].astype(F32))
            es[o] = jnp.where(near == 0, cs[s, o].astype(F32), value).astype(BF16)

        block = es[...].reshape(OPS * ROWS, 2 * NV)
        both = jnp.concatenate([block[:, :NV], block[:, NV:]], axis=0)
        x = nt(both, pg[:, :, s, 0].reshape(NV, NV))
        y = nt(both, pg[:, :, s, 1].reshape(NV, NV))
        wb[0] = (x[: OPS * ROWS] + y[OPS * ROWS :]).reshape(OPS, ROWS, NV)
        wb[1] = (x[OPS * ROWS :] - y[: OPS * ROWS]).reshape(OPS, ROWS, NV)

        @pl.loop(0, OPS)
        def _(a):
            pa = pos[a]
            l_re = lt[pa, 0, s]
            l_im = lt[pa, 1, s]
            for b in range(OPS):
                pb = pos[b]
                w_re = wb[0, pb]
                w_im = wb[1, pb]
                at = s * 72 + a * OPS + b
                red[at] = fold(l_re * w_re - l_im * w_im)
                red[at + 36] = fold(l_re * w_im + l_im * w_re)

    sums = jnp.sum(red[...], axis=1)
    res[r] = nt(jnp.ones((8, 128), F32), sums, lax.Precision.HIGHEST)

    @pl.loop(1, space)
    def _(d):
        ps_copy((r + d) % space, r).start()

    @pl.loop(1, space)
    def _(d):
        ps_copy(r, (r + d) % space).wait_recv()

    total = res[0]
    for q in range(1, space):
        total = total + res[q]
    out_ref[...] = total

    z_copy().wait_send()

    @pl.loop(0, OPS)
    def _(i):
        pair_copy(i).wait_send()
        remote(sb.at[i, pl.ds(0, 7)], sb.at[i, pl.ds(0, 7)], rs_send.at[i], pfr, "space", partner).wait_send()
        remote(et.at[i, pl.ds(0, 112)], et.at[i, pl.ds(0, 112)], ag_send.at[i], pfr, "space", partner).wait_send()
        fw_copy(i, core).wait_send()
        xh_copy(i).wait_send()

    for w in range(2):

        @pl.loop(0, steps[w])
        def _(k):
            remote(rrecv.at[w, 0], rrecv.at[w, 0], bc_send.at[w, k], pfr, "space", partner).wait_send()

    remote(pg.at[pl.ds(0, 7), 0], pg.at[pl.ds(0, 7), 0], pgs, pfr, "space", partner).wait_send()
    pf_copy(core).wait_send()
    remote(res.at[pl.ds(0, 15)], res.at[pl.ds(0, 15)], ps_send, pfr, "space", partner).wait_send()


def fused(ring, v, momenta, displacement, sources, p):
    dma = pltpu.SemaphoreType.DMA
    most = OPS + ring // 2 - 1
    return pl.pallas_call(
        functools.partial(kernel, ring),
        out_shape=jax.ShapeDtypeStruct((8, 384), F32),
        in_specs=[
            pl.BlockSpec(memory_space=pl.ANY),
            pl.BlockSpec(memory_space=pltpu.SMEM),
            pl.BlockSpec(memory_space=pltpu.SMEM),
            pl.BlockSpec(memory_space=pltpu.SMEM),
            pl.BlockSpec(memory_space=pl.ANY),
        ],
        out_specs=pl.BlockSpec(memory_space=pltpu.VMEM),
        scratch_shapes=[
            pltpu.VMEM((3, 6, NV, NV), BF16),
            pltpu.VMEM((6, NV, NV), BF16),
            pltpu.VMEM((NV, 6 * NV), BF16),
            pltpu.VMEM((6 * NV, 2 * NV), BF16),
            pltpu.VMEM((OPS, 2, NV, 128), F32),
            pltpu.VMEM((OPS, NV, 2 * NV), F32),
            pltpu.VMEM((OPS, 128, 2 * NV), F32),
            pltpu.VMEM((OPS, CHIPS, ROWS, 2 * NV), BF16),
            pltpu.VMEM((OPS, CHIPS, ROWS, 2 * NV), BF16),
            pltpu.VMEM((OPS, NV, 2 * NV), BF16),
            pltpu.VMEM((OPS, ROWS, 2 * NV), BF16),
            pltpu.VMEM((SRC, OPS, ROWS, 2 * NV), BF16),
            pltpu.VMEM((2, OPS, SRC, ROWS, 2 * NV), BF16),
            pltpu.VMEM((2, most, SRC, ROWS, 2 * NV), BF16),
            pltpu.VMEM((CHIPS, 2, SRC, 2, ROWS, NV), BF16),
            pltpu.VMEM((128, NV), BF16),
            pltpu.VMEM((OPS, 2, SRC, ROWS, NV), F32),
            pltpu.VMEM((2, OPS, ROWS, NV), F32),
            pltpu.VMEM((OPS, ROWS, 2 * NV), BF16),
            pltpu.VMEM((384, 8, 128), F32),
            pltpu.VMEM((2 * CHIPS, 8, 384), F32),
            pltpu.SMEM((OPS,), jnp.int32),
            pltpu.SMEM((OPS,), jnp.int32),
            pltpu.SMEM((OPS,), jnp.int32),
            dma((2,)),
            dma, dma,
            dma((OPS,)), dma((OPS,)),
            dma((OPS,)), dma((OPS, CHIPS)),
            dma((OPS,)), dma((OPS, CHIPS)),
            dma((OPS,)), dma((OPS,)),
            dma((OPS,)), dma((OPS,)),
            dma((2, most)), dma((2, most, SRC)),
            dma, dma((CHIPS,)),
            dma, dma,
            dma, dma((2 * CHIPS,)),
        ],
        compiler_params=pltpu.CompilerParams(
            collective_id=0, has_side_effects=True, vmem_limit_bytes=48 << 20
        ),
    )(v, momenta, displacement, sources, p)


def body(eigenvectors, momenta, displacement, source_times, perambulators):
    ring = lax.axis_size("tm") // 2
    sums = fused(
        ring,
        eigenvectors.reshape(6, NV, NV),
        momenta,
        displacement,
        source_times,
        perambulators.reshape(SRC, 2, ROWS, NV),
    )
    correlator = sums[0, : SRC * 72].reshape(1, SRC, 2, OPS, OPS)
    diagonal = jnp.diagonal(correlator, axis1=3, axis2=4)
    real = diagonal[:, :, 0]
    imaginary = diagonal[:, :, 1]
    pair_real = real[:, :, :, None] * real[:, :, None, :] - imaginary[:, :, :, None] * imaginary[:, :, None, :]
    pair_imaginary = real[:, :, :, None] * imaginary[:, :, None, :] + imaginary[:, :, :, None] * real[:, :, None, :]
    return (correlator, jnp.stack([pair_real, pair_imaginary], axis=2))


def solution(mesh):
    placed = (
        P("tm", None, None, "space", None, None),
        P(),
        P(),
        P(),
        P("tm", None, None, "space", None),
    )
    return jax.shard_map(
        body,
        mesh=mesh,
        in_specs=placed,
        out_specs=(P("tm", None, None, None, None), P("tm", None, None, None, None)),
        check_vma=False,
    )
```

```python
import functools
import math

import jax
import jax.numpy as jnp
from jax import lax
from jax.experimental import pallas as pl
from jax.experimental.pallas import tpu as pltpu
from jax.sharding import PartitionSpec as P

MESH = pl.DeviceIdType.MESH
F32 = jnp.float32
BF16 = jnp.bfloat16
OPS = 6
SRC = 4
CHIPS = 8
NV = 256
ROWS = 16
COSINE = [math.cos(2.0 * math.pi * m / 16) for m in range(16)]
SINE = [math.sin(2.0 * math.pi * m / 16) for m in range(16)]


def nt(left, right, precision=None):
    return lax.dot_general(
        left, right, (((1,), (1,)), ((), ())), precision=precision, preferred_element_type=F32
    )


def fold(block):
    halves = block[:, :128] + block[:, 128:]
    return halves[:8] + halves[8:]


def kernel(
    ring, v_hbm, mom_hbm, disp_hbm, src_hbm, p_hbm, corr_ref, two_ref,
    sh3, zb, vt, rhs, ctb, part, prt, sb, rsr, xs, xr, et, ga, gb, sel, come, pg, pct, lt, wb, red, res,
    mom, disp, src, perm, pos, dsort,
    loc_sem, zs_send, zs_recv, pr_send, pr_recv, rs_send, rs_recv, xs_send, xs_recv,
    gx_send, gx_recv, gy_send, gy_recv, fw_send, fw_recv, xh_send, xh_recv, hop_send, hop_recv,
    px_send, px_recv, py_send, py_recv, pf_send, pf_recv, ps_send, ps_recv,
):
    space = 2 * CHIPS
    half = ring // 2
    hops = (half, ring - 1 - half)
    rings = (ga, gb)
    r = lax.axis_index("space")
    t = lax.axis_index("tm")
    chip = r // 2
    core = r % 2
    xh = t // ring
    z = t % ring
    partner = 2 * chip + 1 - core
    ahead = (xh * ring + (z + 1) % ring, xh * ring + (z + ring - 1) % ring)
    across = (1 - xh) * ring + z
    own = core * 128 + chip * ROWS

    y = chip // 2
    x = chip % 2
    beside = 2 * (2 * y + 1 - x) + core

    def level(d):
        return (y + d) % 4

    def on_level(q):
        return 2 * (2 * q + x) + core

    def remote(src_ref, dst_ref, send, recv, axis, index):
        return pltpu.make_async_remote_copy(
            src_ref=src_ref, dst_ref=dst_ref, send_sem=send, recv_sem=recv,
            device_id={axis: index}, device_id_type=MESH,
        )

    def rows_of(q):
        return pl.ds(pl.multiple_of(core * 128 + q * 2 * ROWS, 2 * ROWS), 2 * ROWS)

    def own_rows():
        return pl.ds(pl.multiple_of(own, ROWS), ROWS)

    def beside_rows():
        return pl.ds(pl.multiple_of(core * 128 + y * 2 * ROWS + (1 - x) * ROWS, ROWS), ROWS)

    def three(b):
        return pl.ds(3 * b, 3)

    def side(c):
        return pl.ds(pl.multiple_of(c * 128, 128), 128)

    def z_copy():
        return remote(v_hbm, zb, zs_send, zs_recv, "space", (r + space - 1) % space)

    def pair_copy(i):
        return remote(part.at[i, side(1 - core)], prt.at[i], pr_send.at[i], pr_recv.at[i], "space", partner)

    def rs_copy(i, to, frm):
        return remote(sb.at[i, to], rsr.at[i, frm], rs_send.at[i], rs_recv.at[i, frm], "space", on_level(to))

    def xs_copy(i):
        return remote(xs.at[i, 1 - x], xr.at[i], xs_send.at[i], xs_recv.at[i], "space", beside)

    def gx_copy(b, rows):
        part_of = et.at[three(b), rows]
        return remote(part_of, part_of, gx_send.at[b], gx_recv.at[b], "space", beside)

    def gy_copy(b, to, frm):
        part_of = et.at[three(b), rows_of(frm)]
        return remote(part_of, part_of, gy_send.at[b], gy_recv.at[b, frm], "space", on_level(to))

    def fw_copy(b, c):
        part_of = et.at[three(b), side(c)]
        return remote(part_of, part_of, fw_send.at[b], fw_recv.at[b], "space", partner)

    def xh_copy(b):
        return remote(sel.at[b], come.at[b], xh_send.at[b], xh_recv.at[b], "tm", across)

    def hop_copy(b, w, j):
        origin = (z + ring - j + 1) % ring if w == 0 else (z + j - 1) % ring
        slot = rings[b].at[origin]
        return remote(slot, slot, hop_send.at[b, w, j], hop_recv.at[b, w, j], "tm", ahead[w])

    def hop_done(b, w, j):
        origin = (z + ring - j) % ring if w == 0 else (z + j) % ring
        slot = rings[b].at[origin]
        remote(slot, slot, hop_send.at[b, w, j], hop_recv.at[b, w, j], "tm", ahead[w]).wait_recv()

    def px_copy(to):
        return remote(p_hbm, pg.at[2 * y + to, core], px_send, px_recv, "space", beside)

    def py_copy(to, frm):
        part_of = pg.at[pl.ds(2 * frm, 2), core]
        return remote(part_of, part_of, py_send, py_recv.at[frm], "space", on_level(to))

    def pf_copy(c):
        return remote(pg.at[:, c], pg.at[:, c], pf_send, pf_recv, "space", partner)

    def ps_copy(to, frm):
        return remote(res.at[frm], res.at[frm], ps_send, ps_recv.at[frm], "space", to)

    barrier = pltpu.get_barrier_semaphore()
    v_copy = pltpu.make_async_copy(v_hbm, sh3.at[0], loc_sem.at[0])
    v_copy.start()
    p_copy = pltpu.make_async_copy(p_hbm, pg.at[chip, core], loc_sem.at[1])
    p_copy.start()
    small = [
        pltpu.make_async_copy(a, b, loc_sem.at[n])
        for n, (a, b) in enumerate(((mom_hbm, mom), (disp_hbm, disp), (src_hbm, src)), 2)
    ]
    for copy in small:
        copy.start()

    @pl.loop(1, space)
    def _(d):
        pl.semaphore_signal(barrier, inc=1, device_id={"space": (r + d) % space}, device_id_type=MESH)

    for other in (*ahead, across):
        pl.semaphore_signal(barrier, inc=1, device_id={"tm": other}, device_id_type=MESH)
    pl.semaphore_wait(barrier, space + 2)
    z_copy().start()

    for copy in small:
        copy.wait()
    place = []
    for o in range(OPS):
        before = jnp.int32(0)
        for q in range(OPS):
            if q != o:
                low = disp[q] <= disp[o] if q < o else disp[q] < disp[o]
                before = before + jnp.where(low, 1, 0)
        place.append(before)
        pos[o] = before
    for j in range(OPS):
        which = jnp.int32(0)
        for o in range(OPS):
            which = which + jnp.where(place[o] == j, o, 0)
        perm[j] = which
        dsort[j] = disp[which]

    site = lax.broadcasted_iota(jnp.int32, (128, NV), 1)
    line = lax.broadcasted_iota(jnp.int32, (128, NV), 0)
    turns = jnp.zeros((128, NV), jnp.int32)
    for j in range(OPS):
        o = perm[j]
        turns = jnp.where(line == j, mom[0, o] * (site & 15) + mom[1, o] * (site >> 4) + mom[2, o] * r, turns)
    turns = turns & 15
    for a, table in enumerate((COSINE, SINE)):
        values = jnp.zeros((128, NV), F32)
        for m in range(16):
            values = jnp.where(turns == m, F32(table[m]), values)
        flipped = values.T
        for j in range(OPS):
            ctb[j, a] = jnp.broadcast_to(flipped[:, j : j + 1], (NV, 128))

    v_copy.wait()
    row = lax.broadcasted_iota(jnp.int32, (NV, NV), 0)
    wraps = (row & 15) == 15
    for p in range(6):
        wide = sh3[0, p].astype(F32)
        vt[:, p * NV : (p + 1) * NV] = wide.T.astype(BF16)
        sh3[1, p] = jnp.where(wraps, pltpu.roll(wide, 15, 0), pltpu.roll(wide, NV - 1, 0)).astype(BF16)
        sh3[2, p, : NV - 16] = sh3[0, p, 16:]
        sh3[2, p, NV - 16 :] = sh3[0, p, :16]

    def weigh(i, beyond):
        d = dsort[i]
        kept = jnp.minimum(d, 2)

        @pl.loop(0, 12)
        def _(step):
            color = step // 4
            top = pl.multiple_of((step % 4) * 64, 64)
            rows = pl.ds(top, 64)
            re = sh3[kept, color, rows]
            im = sh3[kept, 3 + color, rows]
            re = re.astype(F32)
            im = im.astype(F32)
            if beyond:
                moved = jnp.full((64, NV), d, jnp.int32) == 3
                re = jnp.where(moved, zb[color, rows].astype(F32), re)
                im = jnp.where(moved, zb[3 + color, rows].astype(F32), im)
            cosine = ctb[i, 0, rows]
            sine = ctb[i, 1, rows]
            cosine = jnp.concatenate([cosine, cosine], axis=1)
            sine = jnp.concatenate([sine, sine], axis=1)
            w_re = (cosine * re + sine * im).astype(BF16)
            w_im = (cosine * im - sine * re).astype(BF16)
            upper = pl.ds(pl.multiple_of(color * NV + top, 64), 64)
            lower = pl.ds(pl.multiple_of(3 * NV + color * NV + top, 64), 64)
            rhs[upper, :NV] = w_re
            rhs[upper, NV:] = w_im
            rhs[lower, :NV] = w_im
            rhs[lower, NV:] = -w_re

    def elemental(i, beyond):
        weigh(i, beyond)
        part[i] = jnp.dot(vt[...], rhs[...], preferred_element_type=F32)
        pair_copy(i).start()

    def over_y(i):
        pair_copy(i).wait_recv()
        sb[i] = (part[i, side(core)] + prt[i]).astype(BF16).reshape(4, 2 * ROWS, 2 * NV)
        for d in (2, 1, 3):
            rs_copy(i, level(d), y).start()

    def over_x(i):
        ours = pl.ds(pl.multiple_of(y * 2 * ROWS, 2 * ROWS), 2 * ROWS)
        total = part[i, rows_of(y)] + prt[i, ours]
        for d in (1, 3, 2):
            rs_copy(i, y, level(d)).wait_recv()
            total = total + rsr[i, level(d)].astype(F32)
        xs[i] = total.reshape(2, ROWS, 2 * NV)
        xs_copy(i).start()

    def finish(i, b):
        xs_copy(i).wait_recv()
        value = (xs[i, x] + xr[i]).astype(BF16)
        et[i, own_rows()] = value
        rings[b][z, i - 3 * b] = value

    def batch(first, beyond):
        @pl.loop(first, first + 3)
        def _(i):
            elemental(i, beyond)

            @pl.when(i > first)
            def _():
                over_y(i - 1)

        over_y(first + 2)

    def each(stage, first):
        @pl.loop(first, first + 3)
        def _(i):
            stage(i)

    def start_ring(b):
        for w in range(2):
            hop_copy(b, w, 1).start()

    def hop(j):
        for b in range(2):
            for w in range(2):
                if j <= hops[w]:
                    hop_done(b, w, j)
                    if j < hops[w]:
                        hop_copy(b, w, j + 1).start()

    def choose(b):
        @pl.loop(0, SRC)
        def _(s):
            sel[b, s] = rings[b][src[s] & (ring - 1)]

        xh_copy(b).start()

    def gather_y(b):
        gx_copy(b, beside_rows()).wait_recv()
        for d in (2, 1, 3):
            gy_copy(b, level(d), y).start()

    def gather_core(b):
        for d in (1, 3, 2):
            gy_copy(b, y, level(d)).wait_recv()
        fw_copy(b, core).start()

    batch(0, False)
    each(over_x, 0)
    z_copy().wait_recv()
    batch(3, True)
    each(lambda i: finish(i, 0), 0)
    start_ring(0)
    gx_copy(0, own_rows()).start()
    px_copy(x).start()
    each(over_x, 3)
    each(lambda i: finish(i, 1), 3)
    start_ring(1)
    gx_copy(1, own_rows()).start()
    hop(1)
    gather_y(0)
    gather_y(1)
    p_copy.wait()
    px_copy(1 - x).wait_recv()
    for d in (2, 1, 3):
        py_copy(level(d), y).start()
    hop(2)
    hop(3)
    hop(4)
    gather_core(0)
    gather_core(1)
    hop(5)
    for d in (1, 3, 2):
        py_copy(y, level(d)).wait_recv()
    pf_copy(core).start()
    hop(6)
    pf_copy(1 - core).wait_recv()

    pick = lax.broadcasted_iota(jnp.int32, (ROWS, NV), 0) + own == lax.broadcasted_iota(jnp.int32, (ROWS, NV), 1)
    pick = jnp.where(pick, F32(1), F32(0)).astype(BF16)
    for s in range(SRC):
        for a in range(2):
            block = pg[:, :, s, a].reshape(NV, NV)
            pct[a * 64 + s * ROWS : a * 64 + (s + 1) * ROWS] = nt(pick, block).astype(BF16)

    def left_side(b):
        fw_copy(b, 1 - core).wait_recv()

        @pl.loop(3 * b, 3 * b + 3)
        def _(a):
            u = nt(pct[...], et[a, :, :NV])
            v = nt(pct[...], et[a, :, NV:])
            lt[a, 0] = (u[:64] - v[64:]).reshape(SRC, ROWS, NV)
            lt[a, 1] = (v[:64] + u[64:]).reshape(SRC, ROWS, NV)

    def traces(b):
        @pl.loop(0, SRC)
        def _(s):
            here = jnp.full((3, ROWS, 2 * NV), src[s] // ring, jnp.int32) == xh
            block = jnp.where(here, sel[b, s].astype(F32), come[b, s].astype(F32))
            block = block.astype(BF16).reshape(3 * ROWS, 2 * NV)
            both = jnp.concatenate([block[:, :NV], block[:, NV:]], axis=0)
            u = nt(both, pg[:, :, s, 0].reshape(NV, NV))
            v = nt(both, pg[:, :, s, 1].reshape(NV, NV))
            wb[0] = (u[: 3 * ROWS] + v[3 * ROWS :]).reshape(3, ROWS, NV)
            wb[1] = (u[3 * ROWS :] - v[: 3 * ROWS]).reshape(3, ROWS, NV)

            @pl.loop(0, OPS)
            def _(a):
                l_re = lt[a, 0, s]
                l_im = lt[a, 1, s]
                for q in range(3):
                    w_re = wb[0, q]
                    w_im = wb[1, q]
                    at = s * 72 + a * OPS + 3 * b + q
                    red[at] = fold(l_re * w_re - l_im * w_im)
                    red[at + 36] = fold(l_re * w_im + l_im * w_re)

    left_side(0)
    hop(7)
    left_side(1)
    red[288:] = jnp.zeros((96, 8, 128), F32)
    for b in range(2):
        for w in range(2):
            if hops[w] == half:
                hop_done(b, w, half)
        choose(b)
    for b in range(2):
        xh_copy(b).wait_recv()
        traces(b)

    sums = jnp.sum(red[...], axis=1)
    res[r] = nt(jnp.ones((8, 128), F32), sums, lax.Precision.HIGHEST)

    @pl.loop(1, space)
    def _(d):
        ps_copy((r + d) % space, r).start()

    lane = lax.broadcasted_iota(jnp.int32, (64, 384), 1)
    line = lax.broadcasted_iota(jnp.int32, (64, 384), 0)
    sink = jnp.full((64, 384), -1, jnp.int32)
    for o in range(OPS):
        sink = jnp.where((line & 7) == o, pos[o], sink)
    rows_taken = jnp.where((lane // 36 == line // 8) & ((lane % 36) // 6 == sink), F32(1), F32(0))
    lane = lax.broadcasted_iota(jnp.int32, (384, 128), 1)
    line = lax.broadcasted_iota(jnp.int32, (384, 128), 0)
    source = jnp.full((384, 128), -1, jnp.int32)
    for o in range(OPS):
        source = jnp.where(lane == o, pos[o], source)
    columns_taken = jnp.where(line % 6 == source, F32(1), F32(0))
    equal = lax.broadcasted_iota(jnp.int32, (64, 128), 1) == (lax.broadcasted_iota(jnp.int32, (64, 128), 0) & 7)

    @pl.loop(1, space)
    def _(d):
        ps_copy(r, (r + d) % space).wait_recv()

    total = res[0]
    for q in range(1, space):
        total = total + res[q]
    matrix = lax.dot_general(
        rows_taken * total[:1], columns_taken, (((1,), (0,)), ((), ())),
        precision=lax.Precision.HIGHEST, preferred_element_type=F32,
    )
    diagonal = jnp.where(equal, matrix, F32(0))
    down = jnp.sum(diagonal, axis=1, keepdims=True).reshape(SRC, 2, 8, 1)
    over = jnp.sum(diagonal.reshape(SRC, 2, 8, 128), axis=2, keepdims=True)
    matrix = matrix.reshape(SRC, 2, 8, 128)
    pair = (
        down[:, 0] * over[:, 0] - down[:, 1] * over[:, 1],
        down[:, 0] * over[:, 1] + down[:, 1] * over[:, 0],
    )
    for c in range(2):
        for a in range(OPS):
            corr_ref[:, a, c] = matrix[:, c, a, :OPS]
            two_ref[:, a, c] = pair[c][:, a, :OPS]

    z_copy().wait_send()

    def drain(ref, send):
        remote(ref, ref, send, pf_recv, "space", partner).wait_send()

    @pl.loop(0, OPS)
    def _(i):
        pair_copy(i).wait_send()
        drain(sb.at[i, pl.ds(0, 3)], rs_send.at[i])
        xs_copy(i).wait_send()

    for b in range(2):
        gx_copy(b, own_rows()).wait_send()
        drain(et.at[three(b), pl.ds(0, 96)], gy_send.at[b])
        fw_copy(b, core).wait_send()
        xh_copy(b).wait_send()
        for w in range(2):
            for k in range(1, hops[w] + 1):
                hop_copy(b, w, k).wait_send()

    px_copy(x).wait_send()
    drain(pg.at[pl.ds(0, 6), 0], py_send)
    pf_copy(core).wait_send()
    drain(res.at[pl.ds(0, 15)], ps_send)


def fused(ring, v, momenta, displacement, sources, p):
    dma = pltpu.SemaphoreType.DMA
    most = ring // 2 + 1
    return pl.pallas_call(
        functools.partial(kernel, ring),
        out_shape=[jax.ShapeDtypeStruct((SRC, OPS, 2, OPS), F32)] * 2,
        in_specs=[
            pl.BlockSpec(memory_space=pl.ANY),
            pl.BlockSpec(memory_space=pl.ANY),
            pl.BlockSpec(memory_space=pl.ANY),
            pl.BlockSpec(memory_space=pl.ANY),
            pl.BlockSpec(memory_space=pl.ANY),
        ],
        out_specs=[pl.BlockSpec(memory_space=pltpu.VMEM)] * 2,
        scratch_shapes=[
            pltpu.VMEM((3, 6, NV, NV), BF16),
            pltpu.VMEM((6, NV, NV), BF16),
            pltpu.VMEM((NV, 6 * NV), BF16),
            pltpu.VMEM((6 * NV, 2 * NV), BF16),
            pltpu.VMEM((OPS, 2, NV, 128), F32),
            pltpu.VMEM((OPS, NV, 2 * NV), F32),
            pltpu.VMEM((OPS, 128, 2 * NV), F32),
            pltpu.VMEM((OPS, 4, 2 * ROWS, 2 * NV), BF16),
            pltpu.VMEM((OPS, 4, 2 * ROWS, 2 * NV), BF16),
            pltpu.VMEM((OPS, 2, ROWS, 2 * NV), F32),
            pltpu.VMEM((OPS, ROWS, 2 * NV), F32),
            pltpu.VMEM((OPS, NV, 2 * NV), BF16),
            pltpu.VMEM((ring, 3, ROWS, 2 * NV), BF16),
            pltpu.VMEM((ring, 3, ROWS, 2 * NV), BF16),
            pltpu.VMEM((2, SRC, 3, ROWS, 2 * NV), BF16),
            pltpu.VMEM((2, SRC, 3, ROWS, 2 * NV), BF16),
            pltpu.VMEM((CHIPS, 2, SRC, 2, ROWS, NV), BF16),
            pltpu.VMEM((128, NV), BF16),
            pltpu.VMEM((OPS, 2, SRC, ROWS, NV), F32),
            pltpu.VMEM((2, 3, ROWS, NV), F32),
            pltpu.VMEM((384, 8, 128), F32),
            pltpu.VMEM((2 * CHIPS, 8, 384), F32),
            pltpu.SMEM((3, OPS), jnp.int32),
            pltpu.SMEM((OPS,), jnp.int32),
            pltpu.SMEM((SRC,), jnp.int32),
            pltpu.SMEM((OPS,), jnp.int32),
            pltpu.SMEM((OPS,), jnp.int32),
            pltpu.SMEM((OPS,), jnp.int32),
            dma((5,)),
            dma, dma,
            dma((OPS,)), dma((OPS,)),
            dma((OPS,)), dma((OPS, 4)),
            dma((OPS,)), dma((OPS,)),
            dma((2,)), dma((2,)),
            dma((2,)), dma((2, 4)),
            dma((2,)), dma((2,)),
            dma((2,)), dma((2,)),
            dma((2, 2, most)), dma((2, 2, most)),
            dma, dma,
            dma, dma((4,)),
            dma, dma,
            dma, dma((2 * CHIPS,)),
        ],
        compiler_params=pltpu.CompilerParams(
            collective_id=0, has_side_effects=True
        ),
    )(v, momenta, displacement, sources, p)


def body(eigenvectors, momenta, displacement, source_times, perambulators):
    ring = lax.axis_size("tm") // 2
    outputs = fused(
        ring,
        eigenvectors.reshape(6, NV, NV),
        momenta.T,
        displacement,
        source_times,
        perambulators.reshape(SRC, 2, ROWS, NV),
    )
    return tuple(jnp.transpose(out, (0, 2, 1, 3))[None] for out in outputs)


def solution(mesh):
    placed = (
        P("tm", None, None, "space", None, None),
        P(),
        P(),
        P(),
        P("tm", None, None, "space", None),
    )
    return jax.shard_map(
        body,
        mesh=mesh,
        in_specs=placed,
        out_specs=(P("tm", None, None, None, None), P("tm", None, None, None, None)),
        check_vma=False,
    )
```

```python
import functools
import math

import jax
import jax.numpy as jnp
from jax import lax
from jax.experimental import pallas as pl
from jax.experimental.pallas import tpu as pltpu
from jax.sharding import PartitionSpec as P

MESH = pl.DeviceIdType.MESH
F32 = jnp.float32
BF16 = jnp.bfloat16
OPS = 6
SRC = 4
CHIPS = 8
NV = 256
ROWS = 16
COSINE = [math.cos(2.0 * math.pi * m / 16) for m in range(16)]
SINE = [math.sin(2.0 * math.pi * m / 16) for m in range(16)]


def nt(left, right, precision=None):
    return lax.dot_general(
        left, right, (((1,), (1,)), ((), ())), precision=precision, preferred_element_type=F32
    )


def fold(block):
    halves = block[:, :128] + block[:, 128:]
    return halves[:8] + halves[8:]


def kernel(
    ring, v_hbm, mom_hbm, disp_hbm, src_hbm, p_hbm, corr_ref, two_ref,
    sh3, zb, vt, rhs, ctb, part, prt, sb, rsr, xs, xr, et, ga, gb, sel, come, pg, pct, lt, wb, red, res,
    mom, disp, src, perm, pos, dsort,
    loc_sem, zs_send, zs_recv, pr_send, pr_recv, rs_send, rs_recv, xs_send, xs_recv,
    gx_send, gx_recv, gy_send, gy_recv, fw_send, fw_recv, xh_send, xh_recv, hop_send, hop_recv,
    px_send, px_recv, py_send, py_recv, pf_send, pf_recv, ps_send, ps_recv,
):
    space = 2 * CHIPS
    half = ring // 2
    hops = (half, ring - 1 - half)
    rings = (ga, gb)
    r = lax.axis_index("space")
    t = lax.axis_index("tm")
    chip = r // 2
    core = r % 2
    xh = t // ring
    z = t % ring
    partner = 2 * chip + 1 - core
    ahead = (xh * ring + (z + 1) % ring, xh * ring + (z + ring - 1) % ring)
    across = (1 - xh) * ring + z
    own = core * 128 + chip * ROWS

    y = chip // 2
    x = chip % 2
    beside = 2 * (2 * y + 1 - x) + core

    def level(d):
        return (y + d) % 4

    def on_level(q):
        return 2 * (2 * q + x) + core

    def remote(src_ref, dst_ref, send, recv, axis, index):
        return pltpu.make_async_remote_copy(
            src_ref=src_ref, dst_ref=dst_ref, send_sem=send, recv_sem=recv,
            device_id={axis: index}, device_id_type=MESH,
        )

    def rows_of(q):
        return pl.ds(pl.multiple_of(core * 128 + q * 2 * ROWS, 2 * ROWS), 2 * ROWS)

    def own_rows():
        return pl.ds(pl.multiple_of(own, ROWS), ROWS)

    def beside_rows():
        return pl.ds(pl.multiple_of(core * 128 + y * 2 * ROWS + (1 - x) * ROWS, ROWS), ROWS)

    def three(b):
        return pl.ds(3 * b, 3)

    def side(c):
        return pl.ds(pl.multiple_of(c * 128, 128), 128)

    def z_copy(p):
        return remote(v_hbm.at[p], zb.at[p], zs_send.at[p], zs_recv.at[p], "space", (r + space - 1) % space)

    def pair_copy(i):
        return remote(part.at[i, side(1 - core)], prt.at[i], pr_send.at[i], pr_recv.at[i], "space", partner)

    def rs_copy(i, to, frm):
        return remote(sb.at[i, to], rsr.at[i, frm], rs_send.at[i], rs_recv.at[i, frm], "space", on_level(to))

    def xs_copy(i):
        return remote(xs.at[i, 1 - x], xr.at[i], xs_send.at[i], xs_recv.at[i], "space", beside)

    def gx_copy(b, rows):
        part_of = et.at[three(b), rows]
        return remote(part_of, part_of, gx_send.at[b], gx_recv.at[b], "space", beside)

    def gy_copy(b, to, frm):
        part_of = et.at[three(b), rows_of(frm)]
        return remote(part_of, part_of, gy_send.at[b], gy_recv.at[b, frm], "space", on_level(to))

    def fw_copy(b, c):
        part_of = et.at[three(b), side(c)]
        return remote(part_of, part_of, fw_send.at[b], fw_recv.at[b], "space", partner)

    def xh_copy(b, s):
        return remote(sel.at[b, s], come.at[b, s], xh_send.at[b], xh_recv.at[b, s], "tm", across)

    def hop_copy(b, w, j):
        origin = (z + ring - j + 1) % ring if w == 0 else (z + j - 1) % ring
        slot = rings[b].at[origin]
        return remote(slot, slot, hop_send.at[b, w, j], hop_recv.at[b, w, j], "tm", ahead[w])

    def hop_done(b, w, j):
        origin = (z + ring - j) % ring if w == 0 else (z + j) % ring
        slot = rings[b].at[origin]
        remote(slot, slot, hop_send.at[b, w, j], hop_recv.at[b, w, j], "tm", ahead[w]).wait_recv()

    def px_copy(to):
        return remote(p_hbm, pg.at[2 * y + to, core], px_send, px_recv, "space", beside)

    def py_copy(to, frm):
        part_of = pg.at[pl.ds(2 * frm, 2), core]
        return remote(part_of, part_of, py_send, py_recv.at[frm], "space", on_level(to))

    def pf_copy(c):
        return remote(pg.at[:, c], pg.at[:, c], pf_send, pf_recv, "space", partner)

    def ps_copy(to, frm):
        return remote(res.at[frm], res.at[frm], ps_send, ps_recv.at[frm], "space", to)

    barrier = pltpu.get_barrier_semaphore()
    v_copy = pltpu.make_async_copy(v_hbm, sh3.at[0], loc_sem.at[0])
    v_copy.start()
    p_copy = pltpu.make_async_copy(p_hbm, pg.at[chip, core], loc_sem.at[1])
    p_copy.start()
    small = [
        pltpu.make_async_copy(a, b, loc_sem.at[n])
        for n, (a, b) in enumerate(((mom_hbm, mom), (disp_hbm, disp), (src_hbm, src)), 2)
    ]
    for copy in small:
        copy.start()

    @pl.loop(1, space)
    def _(d):
        pl.semaphore_signal(barrier, inc=1, device_id={"space": (r + d) % space}, device_id_type=MESH)

    for other in (*ahead, across):
        pl.semaphore_signal(barrier, inc=1, device_id={"tm": other}, device_id_type=MESH)

    for copy in small:
        copy.wait()
    place = []
    for o in range(OPS):
        before = jnp.int32(0)
        for q in range(OPS):
            if q != o:
                low = disp[q] <= disp[o] if q < o else disp[q] < disp[o]
                before = before + jnp.where(low, 1, 0)
        place.append(before)
        pos[o] = before
    for j in range(OPS):
        which = jnp.int32(0)
        for o in range(OPS):
            which = which + jnp.where(place[o] == j, o, 0)
        perm[j] = which
        dsort[j] = disp[which]

    site = lax.broadcasted_iota(jnp.int32, (128, NV), 1)
    line = lax.broadcasted_iota(jnp.int32, (128, NV), 0)
    turns = jnp.zeros((128, NV), jnp.int32)
    for j in range(OPS):
        o = perm[j]
        turns = jnp.where(line == j, mom[0, o] * (site & 15) + mom[1, o] * (site >> 4) + mom[2, o] * r, turns)
    turns = turns & 15
    for a, table in enumerate((COSINE, SINE)):
        values = jnp.zeros((128, NV), F32)
        for m in range(16):
            values = jnp.where(turns == m, F32(table[m]), values)
        flipped = values.T
        for j in range(OPS):
            ctb[j, a] = jnp.broadcast_to(flipped[:, j : j + 1], (NV, 128))

    v_copy.wait()
    row = lax.broadcasted_iota(jnp.int32, (NV, NV), 0)
    wraps = (row & 15) == 15
    for p in range(6):
        wide = sh3[0, p].astype(F32)
        vt[:, p * NV : (p + 1) * NV] = wide.T.astype(BF16)
        sh3[1, p] = jnp.where(wraps, pltpu.roll(wide, 15, 0), pltpu.roll(wide, NV - 1, 0)).astype(BF16)
        sh3[2, p, : NV - 16] = sh3[0, p, 16:]
        sh3[2, p, NV - 16 :] = sh3[0, p, :16]

    pl.semaphore_wait(barrier, space + 2)
    for color in range(3):
        z_copy(color).start()
        z_copy(3 + color).start()

    def weigh(i, color, beyond):
        d = dsort[i]
        kept = jnp.minimum(d, 2)

        @pl.loop(0, 4)
        def _(part_of):
            top = pl.multiple_of(part_of * 64, 64)
            rows = pl.ds(top, 64)
            re = sh3[kept, color, rows].astype(F32)
            im = sh3[kept, 3 + color, rows].astype(F32)
            if beyond:
                moved = jnp.full((64, NV), d, jnp.int32) == 3
                re = jnp.where(moved, zb[color, rows].astype(F32), re)
                im = jnp.where(moved, zb[3 + color, rows].astype(F32), im)
            cosine = ctb[i, 0, rows]
            sine = ctb[i, 1, rows]
            cosine = jnp.concatenate([cosine, cosine], axis=1)
            sine = jnp.concatenate([sine, sine], axis=1)
            w_re = (cosine * re + sine * im).astype(BF16)
            w_im = (cosine * im - sine * re).astype(BF16)
            upper = pl.ds(pl.multiple_of(color * NV + top, 64), 64)
            lower = pl.ds(pl.multiple_of((3 + color) * NV + top, 64), 64)
            rhs[upper, :NV] = w_re
            rhs[upper, NV:] = w_im
            rhs[lower, :NV] = w_im
            rhs[lower, NV:] = -w_re

    def color_sum(color):
        return sum(
            jnp.dot(
                vt[:, p * NV : (p + 1) * NV], rhs[p * NV : (p + 1) * NV], preferred_element_type=F32
            )
            for p in (color, 3 + color)
        )

    def over_y(i):
        pair_copy(i).wait_recv()
        sb[i] = (part[i, side(core)] + prt[i]).astype(BF16).reshape(4, 2 * ROWS, 2 * NV)
        for d in (2, 1, 3):
            rs_copy(i, level(d), y).start()

    def over_x(i):
        ours = pl.ds(pl.multiple_of(y * 2 * ROWS, 2 * ROWS), 2 * ROWS)
        total = part[i, rows_of(y)] + prt[i, ours]
        for d in (1, 3, 2):
            rs_copy(i, y, level(d)).wait_recv()
            total = total + rsr[i, level(d)].astype(F32)
        xs[i] = total.reshape(2, ROWS, 2 * NV)
        xs_copy(i).start()

    def finish(i, b):
        xs_copy(i).wait_recv()
        value = (xs[i, x] + xr[i]).astype(BF16)
        et[i, own_rows()] = value
        rings[b][z, i - 3 * b] = value

    def sent(i, first):
        pair_copy(i).start()

        @pl.when(i > first)
        def _():
            over_y(i - 1)

    def near_batch():
        @pl.loop(0, 3)
        def _(i):
            @pl.loop(0, 3)
            def _(color):
                weigh(i, color, False)

            part[i] = jnp.dot(vt[...], rhs[...], preferred_element_type=F32)
            sent(i, 0)

        over_y(2)

    def far_batch(color):
        z_copy(color).wait_recv()
        z_copy(3 + color).wait_recv()

        @pl.loop(3, OPS)
        def _(i):
            weigh(i, color, True)
            if color == 0:
                part[i] = color_sum(color)
            else:
                part[i] += color_sum(color)
            if color == 2:
                sent(i, 3)

        if color == 2:
            over_y(OPS - 1)

    def each(stage, first):
        @pl.loop(first, first + 3)
        def _(i):
            stage(i)

    def start_ring(b):
        for w in range(2):
            hop_copy(b, w, 1).start()

    def hop(b, j):
        for w in range(2):
            if j <= hops[w]:
                hop_done(b, w, j)
                if j < hops[w]:
                    hop_copy(b, w, j + 1).start()

    def choose(b):
        @pl.loop(0, SRC)
        def _(s):
            sel[b, s] = rings[b][src[s] & (ring - 1)]
            xh_copy(b, s).start()

    def gather_y(b):
        gx_copy(b, beside_rows()).wait_recv()
        for d in (2, 1, 3):
            gy_copy(b, level(d), y).start()

    def gather_core(b):
        for d in (1, 3, 2):
            gy_copy(b, y, level(d)).wait_recv()
        fw_copy(b, core).start()

    near_batch()
    far_batch(0)
    far_batch(1)
    far_batch(2)
    each(over_x, 0)
    each(lambda i: finish(i, 0), 0)
    start_ring(0)
    each(over_x, 3)
    hop(0, 1)
    each(lambda i: finish(i, 1), 3)
    start_ring(1)
    gx_copy(0, own_rows()).start()
    gx_copy(1, own_rows()).start()
    px_copy(x).start()
    hop(0, 2)
    hop(1, 1)
    hop(0, 3)
    hop(1, 2)
    gather_y(0)
    gather_y(1)
    p_copy.wait()
    px_copy(1 - x).wait_recv()
    for d in (2, 1, 3):
        py_copy(level(d), y).start()
    hop(0, 4)
    hop(1, 3)
    hop(0, 5)
    hop(1, 4)
    hop(0, 6)
    hop(1, 5)
    hop(0, 7)
    hop(1, 6)
    gather_core(0)
    gather_core(1)
    hop(0, 8)
    choose(0)
    hop(1, 7)
    for d in (1, 3, 2):
        py_copy(y, level(d)).wait_recv()
    pf_copy(core).start()
    red[288:] = jnp.zeros((96, 8, 128), F32)
    hop(1, 8)
    choose(1)
    pf_copy(1 - core).wait_recv()

    pick = lax.broadcasted_iota(jnp.int32, (ROWS, NV), 0) + own == lax.broadcasted_iota(jnp.int32, (ROWS, NV), 1)
    pick = jnp.where(pick, F32(1), F32(0)).astype(BF16)
    for s in range(SRC):
        for a in range(2):
            block = pg[:, :, s, a].reshape(NV, NV)
            pct[a * 64 + s * ROWS : a * 64 + (s + 1) * ROWS] = nt(pick, block).astype(BF16)

    def left_side(b):
        fw_copy(b, 1 - core).wait_recv()

        @pl.loop(3 * b, 3 * b + 3)
        def _(a):
            u = nt(pct[...], et[a, :, :NV])
            v = nt(pct[...], et[a, :, NV:])
            lt[a, 0] = (u[:64] - v[64:]).reshape(SRC, ROWS, NV)
            lt[a, 1] = (v[:64] + u[64:]).reshape(SRC, ROWS, NV)

    def traces(b):
        @pl.loop(0, SRC)
        def _(s):
            xh_copy(b, s).wait_recv()
            here = jnp.full((3, ROWS, 2 * NV), src[s] // ring, jnp.int32) == xh
            block = jnp.where(here, sel[b, s].astype(F32), come[b, s].astype(F32))
            block = block.astype(BF16).reshape(3 * ROWS, 2 * NV)
            both = jnp.concatenate([block[:, :NV], block[:, NV:]], axis=0)
            u = nt(both, pg[:, :, s, 0].reshape(NV, NV))
            v = nt(both, pg[:, :, s, 1].reshape(NV, NV))
            wb[0] = (u[: 3 * ROWS] + v[3 * ROWS :]).reshape(3, ROWS, NV)
            wb[1] = (u[3 * ROWS :] - v[: 3 * ROWS]).reshape(3, ROWS, NV)

            @pl.loop(0, OPS)
            def _(a):
                l_re = lt[a, 0, s]
                l_im = lt[a, 1, s]
                for q in range(3):
                    w_re = wb[0, q]
                    w_im = wb[1, q]
                    at = s * 72 + a * OPS + 3 * b + q
                    red[at] = fold(l_re * w_re - l_im * w_im)
                    red[at + 36] = fold(l_re * w_im + l_im * w_re)

    left_side(0)
    left_side(1)
    traces(0)
    traces(1)

    sums = jnp.sum(red[...], axis=1)
    res[r] = nt(jnp.ones((8, 128), F32), sums, lax.Precision.HIGHEST)[:1]

    @pl.loop(1, space)
    def _(d):
        ps_copy((r + d) % space, r).start()

    lane = lax.broadcasted_iota(jnp.int32, (64, 384), 1)
    line = lax.broadcasted_iota(jnp.int32, (64, 384), 0)
    sink = jnp.full((64, 384), -1, jnp.int32)
    for o in range(OPS):
        sink = jnp.where((line & 7) == o, pos[o], sink)
    rows_taken = jnp.where((lane // 36 == line // 8) & ((lane % 36) // 6 == sink), F32(1), F32(0))
    lane = lax.broadcasted_iota(jnp.int32, (384, 128), 1)
    line = lax.broadcasted_iota(jnp.int32, (384, 128), 0)
    source = jnp.full((384, 128), -1, jnp.int32)
    for o in range(OPS):
        source = jnp.where(lane == o, pos[o], source)
    columns_taken = jnp.where(line % 6 == source, F32(1), F32(0))
    equal = lax.broadcasted_iota(jnp.int32, (64, 128), 1) == (lax.broadcasted_iota(jnp.int32, (64, 128), 0) & 7)

    @pl.loop(1, space)
    def _(d):
        ps_copy(r, (r + d) % space).wait_recv()

    total = res[0]
    for q in range(1, space):
        total = total + res[q]
    matrix = lax.dot_general(
        rows_taken * total, columns_taken, (((1,), (0,)), ((), ())),
        precision=lax.Precision.HIGHEST, preferred_element_type=F32,
    )
    diagonal = jnp.where(equal, matrix, F32(0))
    down = jnp.sum(diagonal, axis=1, keepdims=True).reshape(SRC, 2, 8, 1)
    over = jnp.sum(diagonal.reshape(SRC, 2, 8, 128), axis=2, keepdims=True)
    matrix = matrix.reshape(SRC, 2, 8, 128)
    pair = (
        down[:, 0] * over[:, 0] - down[:, 1] * over[:, 1],
        down[:, 0] * over[:, 1] + down[:, 1] * over[:, 0],
    )
    for c in range(2):
        for a in range(OPS):
            corr_ref[:, a, c] = matrix[:, c, a, :OPS]
            two_ref[:, a, c] = pair[c][:, a, :OPS]

    for p in range(6):
        z_copy(p).wait_send()

    def drain(ref, send):
        remote(ref, ref, send, pf_recv, "space", partner).wait_send()

    @pl.loop(0, OPS)
    def _(i):
        pair_copy(i).wait_send()
        drain(sb.at[i, pl.ds(0, 3)], rs_send.at[i])
        xs_copy(i).wait_send()

    for b in range(2):
        gx_copy(b, own_rows()).wait_send()
        drain(et.at[three(b), pl.ds(0, 96)], gy_send.at[b])
        fw_copy(b, core).wait_send()
        drain(sel.at[b], xh_send.at[b])
        for w in range(2):
            for k in range(1, hops[w] + 1):
                hop_copy(b, w, k).wait_send()

    px_copy(x).wait_send()
    drain(pg.at[pl.ds(0, 6), 0], py_send)
    pf_copy(core).wait_send()
    drain(res.at[pl.ds(0, 15)], ps_send)


def fused(ring, v, momenta, displacement, sources, p):
    dma = pltpu.SemaphoreType.DMA
    most = ring // 2 + 1
    return pl.pallas_call(
        functools.partial(kernel, ring),
        out_shape=[jax.ShapeDtypeStruct((SRC, OPS, 2, OPS), F32)] * 2,
        in_specs=[
            pl.BlockSpec(memory_space=pl.ANY),
            pl.BlockSpec(memory_space=pl.ANY),
            pl.BlockSpec(memory_space=pl.ANY),
            pl.BlockSpec(memory_space=pl.ANY),
            pl.BlockSpec(memory_space=pl.ANY),
        ],
        out_specs=[pl.BlockSpec(memory_space=pltpu.VMEM)] * 2,
        scratch_shapes=[
            pltpu.VMEM((3, 6, NV, NV), BF16),
            pltpu.VMEM((6, NV, NV), BF16),
            pltpu.VMEM((NV, 6 * NV), BF16),
            pltpu.VMEM((6 * NV, 2 * NV), BF16),
            pltpu.VMEM((OPS, 2, NV, 128), F32),
            pltpu.VMEM((OPS, NV, 2 * NV), F32),
            pltpu.VMEM((OPS, 128, 2 * NV), F32),
            pltpu.VMEM((OPS, 4, 2 * ROWS, 2 * NV), BF16),
            pltpu.VMEM((OPS, 4, 2 * ROWS, 2 * NV), BF16),
            pltpu.VMEM((OPS, 2, ROWS, 2 * NV), F32),
            pltpu.VMEM((OPS, ROWS, 2 * NV), F32),
            pltpu.VMEM((OPS, NV, 2 * NV), BF16),
            pltpu.VMEM((ring, 3, ROWS, 2 * NV), BF16),
            pltpu.VMEM((ring, 3, ROWS, 2 * NV), BF16),
            pltpu.VMEM((2, SRC, 3, ROWS, 2 * NV), BF16),
            pltpu.VMEM((2, SRC, 3, ROWS, 2 * NV), BF16),
            pltpu.VMEM((CHIPS, 2, SRC, 2, ROWS, NV), BF16),
            pltpu.VMEM((128, NV), BF16),
            pltpu.VMEM((OPS, 2, SRC, ROWS, NV), F32),
            pltpu.VMEM((2, 3, ROWS, NV), F32),
            pltpu.VMEM((384, 8, 128), F32),
            pltpu.VMEM((2 * CHIPS, 1, 384), F32),
            pltpu.SMEM((3, OPS), jnp.int32),
            pltpu.SMEM((OPS,), jnp.int32),
            pltpu.SMEM((SRC,), jnp.int32),
            pltpu.SMEM((OPS,), jnp.int32),
            pltpu.SMEM((OPS,), jnp.int32),
            pltpu.SMEM((OPS,), jnp.int32),
            dma((5,)),
            dma((6,)), dma((6,)),
            dma((OPS,)), dma((OPS,)),
            dma((OPS,)), dma((OPS, 4)),
            dma((OPS,)), dma((OPS,)),
            dma((2,)), dma((2,)),
            dma((2,)), dma((2, 4)),
            dma((2,)), dma((2,)),
            dma((2,)), dma((2, SRC)),
            dma((2, 2, most)), dma((2, 2, most)),
            dma, dma,
            dma, dma((4,)),
            dma, dma,
            dma, dma((2 * CHIPS,)),
        ],
        compiler_params=pltpu.CompilerParams(
            collective_id=0, has_side_effects=True
        ),
    )(v, momenta, displacement, sources, p)


def body(eigenvectors, momenta, displacement, source_times, perambulators):
    ring = lax.axis_size("tm") // 2
    outputs = fused(
        ring,
        eigenvectors.reshape(6, NV, NV),
        momenta.T,
        displacement,
        source_times,
        perambulators.reshape(SRC, 2, ROWS, NV),
    )
    return tuple(jnp.transpose(out, (0, 2, 1, 3))[None] for out in outputs)


def solution(mesh):
    placed = (
        P("tm", None, None, "space", None, None),
        P(),
        P(),
        P(),
        P("tm", None, None, "space", None),
    )
    return jax.shard_map(
        body,
        mesh=mesh,
        in_specs=placed,
        out_specs=(P("tm", None, None, None, None), P("tm", None, None, None, None)),
        check_vma=False,
    )
```

```python
import functools
import math

import jax
import jax.numpy as jnp
from jax import lax
from jax.experimental import pallas as pl
from jax.experimental.pallas import tpu as pltpu
from jax.sharding import PartitionSpec as P

MESH = pl.DeviceIdType.MESH
F32 = jnp.float32
BF16 = jnp.bfloat16
OPS = 6
SRC = 4
CHIPS = 8
NV = 256
ROWS = 16
COSINE = [math.cos(2.0 * math.pi * m / 16) for m in range(16)]
SINE = [math.sin(2.0 * math.pi * m / 16) for m in range(16)]


def nt(left, right, precision=None):
    return lax.dot_general(
        left, right, (((1,), (1,)), ((), ())), precision=precision, preferred_element_type=F32
    )


def fold(block):
    halves = block[:, :128] + block[:, 128:]
    return halves[:8] + halves[8:]


def kernel(
    ring, v_hbm, mom_hbm, disp_hbm, src_hbm, p_hbm, corr_ref, two_ref,
    sh3, zb, zr, vt, rhs, ctb, part, prt, sb, rsr, xs, xr, et, ga, gb, sel, come, pg, pct, lt, wb, red, res,
    mom, disp, src, perm, pos, dsort,
    loc_sem, zs_send, zs_recv, zr_send, zr_recv, pr_send, pr_recv, rs_send, rs_recv, xs_send, xs_recv,
    gx_send, gx_recv, gy_send, gy_recv, fw_send, fw_recv, xh_send, xh_recv, hop_send, hop_recv,
    px_send, px_recv, py_send, py_recv, pf_send, pf_recv, ps_send, ps_recv,
):
    space = 2 * CHIPS
    half = ring // 2
    hops = (half, ring - 1 - half)
    rings = (ga, gb)
    r = lax.axis_index("space")
    t = lax.axis_index("tm")
    chip = r // 2
    core = r % 2
    xh = t // ring
    z = t % ring
    partner = 2 * chip + 1 - core
    ahead = (xh * ring + (z + 1) % ring, xh * ring + (z + ring - 1) % ring)
    across = (1 - xh) * ring + z
    own = core * 128 + chip * ROWS

    y = chip // 2
    x = chip % 2
    beside = 2 * (2 * y + 1 - x) + core

    def level(d):
        return (y + d) % 4

    def on_level(q):
        return 2 * (2 * q + x) + core

    def remote(src_ref, dst_ref, send, recv, axis, index):
        return pltpu.make_async_remote_copy(
            src_ref=src_ref, dst_ref=dst_ref, send_sem=send, recv_sem=recv,
            device_id={axis: index}, device_id_type=MESH,
        )

    def rows_of(q):
        return pl.ds(pl.multiple_of(core * 128 + q * 2 * ROWS, 2 * ROWS), 2 * ROWS)

    def own_rows():
        return pl.ds(pl.multiple_of(own, ROWS), ROWS)

    def beside_rows():
        return pl.ds(pl.multiple_of(core * 128 + y * 2 * ROWS + (1 - x) * ROWS, ROWS), ROWS)

    def three(b):
        return pl.ds(3 * b, 3)

    def side(c):
        return pl.ds(pl.multiple_of(c * 128, 128), 128)

    def z_copy(p):
        return remote(sh3.at[0, p], zb.at[p], zs_send.at[p], zs_recv.at[p], "space", (r + space - 1) % space)

    relays = (x == 0) & (core == 0)

    def zr_copy(n):
        return remote(sh3.at[0, 2 + 3 * n], zr.at[n], zr_send.at[n], zr_recv.at[n], "space", (r + space - 4) % space)

    def pass_on(n):
        return remote(zr.at[n], zb.at[2 + 3 * n], zs_send.at[2 + 3 * n], zs_recv.at[2 + 3 * n], "space", (r + 3) % space)

    def pair_copy(i):
        return remote(part.at[i, side(1 - core)], prt.at[i], pr_send.at[i], pr_recv.at[i], "space", partner)

    def rs_copy(i, to, frm):
        return remote(sb.at[i, to], rsr.at[i, frm], rs_send.at[i], rs_recv.at[i, frm], "space", on_level(to))

    def xs_copy(i):
        return remote(xs.at[i, 1 - x], xr.at[i], xs_send.at[i], xs_recv.at[i], "space", beside)

    def gx_copy(b, rows):
        part_of = et.at[three(b), rows]
        return remote(part_of, part_of, gx_send.at[b], gx_recv.at[b], "space", beside)

    def gy_copy(b, to, frm):
        part_of = et.at[three(b), rows_of(frm)]
        return remote(part_of, part_of, gy_send.at[b], gy_recv.at[b, frm], "space", on_level(to))

    def fw_copy(b, c):
        part_of = et.at[three(b), side(c)]
        return remote(part_of, part_of, fw_send.at[b], fw_recv.at[b], "space", partner)

    def xh_copy(b, s):
        return remote(sel.at[b, s], come.at[b, s], xh_send.at[b], xh_recv.at[b, s], "tm", across)

    def hop_copy(b, w, j):
        origin = (z + ring - j + 1) % ring if w == 0 else (z + j - 1) % ring
        slot = rings[b].at[origin]
        return remote(slot, slot, hop_send.at[b, w, j], hop_recv.at[b, w, j], "tm", ahead[w])

    def hop_done(b, w, j):
        origin = (z + ring - j) % ring if w == 0 else (z + j) % ring
        slot = rings[b].at[origin]
        remote(slot, slot, hop_send.at[b, w, j], hop_recv.at[b, w, j], "tm", ahead[w]).wait_recv()

    def px_copy(to):
        return remote(p_hbm, pg.at[2 * y + to, core], px_send, px_recv, "space", beside)

    def py_copy(to, frm):
        part_of = pg.at[pl.ds(2 * frm, 2), core]
        return remote(part_of, part_of, py_send, py_recv.at[frm], "space", on_level(to))

    def pf_copy(c):
        return remote(pg.at[:, c], pg.at[:, c], pf_send, pf_recv, "space", partner)

    def ps_copy(to, frm):
        return remote(res.at[frm], res.at[frm], ps_send, ps_recv.at[frm], "space", to)

    barrier = pltpu.get_barrier_semaphore()
    v_copy = pltpu.make_async_copy(v_hbm, sh3.at[0], loc_sem.at[0])
    v_copy.start()
    p_copy = pltpu.make_async_copy(p_hbm, pg.at[chip, core], loc_sem.at[1])
    p_copy.start()
    small = [
        pltpu.make_async_copy(a, b, loc_sem.at[n])
        for n, (a, b) in enumerate(((mom_hbm, mom), (disp_hbm, disp), (src_hbm, src)), 2)
    ]
    for copy in small:
        copy.start()

    @pl.loop(1, space)
    def _(d):
        pl.semaphore_signal(barrier, inc=1, device_id={"space": (r + d) % space}, device_id_type=MESH)

    for other in (*ahead, across):
        pl.semaphore_signal(barrier, inc=1, device_id={"tm": other}, device_id_type=MESH)

    v_copy.wait()
    pl.semaphore_wait(barrier, space + 2)

    @pl.when(relays)
    def _():
        for n in range(2):
            zr_copy(n).start()

    for color in range(2):
        z_copy(color).start()
        z_copy(3 + color).start()

    @pl.when(jnp.logical_not(relays))
    def _():
        z_copy(2).start()
        z_copy(5).start()

    for copy in small:
        copy.wait()
    place = []
    for o in range(OPS):
        before = jnp.int32(0)
        for q in range(OPS):
            if q != o:
                low = disp[q] <= disp[o] if q < o else disp[q] < disp[o]
                before = before + jnp.where(low, 1, 0)
        place.append(before)
        pos[o] = before
    for j in range(OPS):
        which = jnp.int32(0)
        for o in range(OPS):
            which = which + jnp.where(place[o] == j, o, 0)
        perm[j] = which
        dsort[j] = disp[which]

    site = lax.broadcasted_iota(jnp.int32, (128, NV), 1)
    line = lax.broadcasted_iota(jnp.int32, (128, NV), 0)
    turns = jnp.zeros((128, NV), jnp.int32)
    for j in range(OPS):
        o = perm[j]
        turns = jnp.where(line == j, mom[0, o] * (site & 15) + mom[1, o] * (site >> 4) + mom[2, o] * r, turns)
    turns = turns & 15
    for a, table in enumerate((COSINE, SINE)):
        values = jnp.zeros((128, NV), F32)
        for m in range(16):
            values = jnp.where(turns == m, F32(table[m]), values)
        flipped = values.T
        for j in range(OPS):
            ctb[j, a] = jnp.broadcast_to(flipped[:, j : j + 1], (NV, 128))

    row = lax.broadcasted_iota(jnp.int32, (NV, NV), 0)
    wraps = (row & 15) == 15
    for p in range(6):
        wide = sh3[0, p].astype(F32)
        vt[:, p * NV : (p + 1) * NV] = wide.T.astype(BF16)
        sh3[1, p] = jnp.where(wraps, pltpu.roll(wide, 15, 0), pltpu.roll(wide, NV - 1, 0)).astype(BF16)
        sh3[2, p, : NV - 16] = sh3[0, p, 16:]
        sh3[2, p, NV - 16 :] = sh3[0, p, :16]

    def weigh(i, color, beyond):
        d = dsort[i]
        kept = jnp.minimum(d, 2)

        @pl.loop(0, 4)
        def _(part_of):
            top = pl.multiple_of(part_of * 64, 64)
            rows = pl.ds(top, 64)
            re = sh3[kept, color, rows].astype(F32)
            im = sh3[kept, 3 + color, rows].astype(F32)
            if beyond:
                moved = jnp.full((64, NV), d, jnp.int32) == 3
                re = jnp.where(moved, zb[color, rows].astype(F32), re)
                im = jnp.where(moved, zb[3 + color, rows].astype(F32), im)
            cosine = ctb[i, 0, rows]
            sine = ctb[i, 1, rows]
            cosine = jnp.concatenate([cosine, cosine], axis=1)
            sine = jnp.concatenate([sine, sine], axis=1)
            w_re = (cosine * re + sine * im).astype(BF16)
            w_im = (cosine * im - sine * re).astype(BF16)
            upper = pl.ds(pl.multiple_of(color * NV + top, 64), 64)
            lower = pl.ds(pl.multiple_of((3 + color) * NV + top, 64), 64)
            rhs[upper, :NV] = w_re
            rhs[upper, NV:] = w_im
            rhs[lower, :NV] = w_im
            rhs[lower, NV:] = -w_re

    def color_sum(color):
        return sum(
            jnp.dot(
                vt[:, p * NV : (p + 1) * NV], rhs[p * NV : (p + 1) * NV], preferred_element_type=F32
            )
            for p in (color, 3 + color)
        )

    def over_y(i):
        pair_copy(i).wait_recv()
        sb[i] = (part[i, side(core)] + prt[i]).astype(BF16).reshape(4, 2 * ROWS, 2 * NV)
        for d in (2, 1, 3):
            rs_copy(i, level(d), y).start()

    def over_x(i):
        ours = pl.ds(pl.multiple_of(y * 2 * ROWS, 2 * ROWS), 2 * ROWS)
        total = part[i, rows_of(y)] + prt[i, ours]
        for d in (1, 3, 2):
            rs_copy(i, y, level(d)).wait_recv()
            total = total + rsr[i, level(d)].astype(F32)
        xs[i] = total.reshape(2, ROWS, 2 * NV)
        xs_copy(i).start()

    def finish(i, b):
        xs_copy(i).wait_recv()
        value = (xs[i, x] + xr[i]).astype(BF16)
        et[i, own_rows()] = value
        rings[b][z, i - 3 * b] = value

    def near_batch():
        @pl.loop(0, 3)
        def _(i):
            @pl.loop(0, 3)
            def _(color):
                weigh(i, color, False)

            part[i] = jnp.dot(vt[...], rhs[...], preferred_element_type=F32)
            pair_copy(i).start()

    def far_batch(color):
        z_copy(color).wait_recv()
        z_copy(3 + color).wait_recv()

        @pl.loop(3, OPS)
        def _(i):
            weigh(i, color, True)
            if color == 0:
                part[i] = color_sum(color)
            else:
                part[i] += color_sum(color)
            if color == 2:
                pair_copy(i).start()

    def each(stage, first):
        @pl.loop(first, first + 3)
        def _(i):
            stage(i)

    def start_ring(b):
        for w in range(2):
            hop_copy(b, w, 1).start()

    def hop(b, j):
        for w in range(2):
            if j <= hops[w]:
                hop_done(b, w, j)
                if j < hops[w]:
                    hop_copy(b, w, j + 1).start()

    def choose(b):
        @pl.loop(0, SRC)
        def _(s):
            sel[b, s] = rings[b][src[s] & (ring - 1)]
            xh_copy(b, s).start()

    def gather_y(b):
        gx_copy(b, beside_rows()).wait_recv()
        for d in (2, 1, 3):
            gy_copy(b, level(d), y).start()

    def gather_core(b):
        for d in (1, 3, 2):
            gy_copy(b, y, level(d)).wait_recv()
        fw_copy(b, core).start()

    near_batch()

    @pl.when(relays)
    def _():
        for n in range(2):
            zr_copy(n).wait_recv()
            pass_on(n).start()

    far_batch(0)
    each(over_y, 0)
    far_batch(1)
    far_batch(2)

    @pl.when(core == 0)
    def _():
        each(over_x, 0)

    each(over_y, 3)

    @pl.when(core == 1)
    def _():
        each(over_x, 0)

    each(lambda i: finish(i, 0), 0)
    start_ring(0)
    each(over_x, 3)
    hop(0, 1)
    each(lambda i: finish(i, 1), 3)
    start_ring(1)
    gx_copy(0, own_rows()).start()
    gx_copy(1, own_rows()).start()
    px_copy(x).start()
    hop(0, 2)
    hop(1, 1)
    p_copy.wait()
    px_copy(1 - x).wait_recv()
    for d in (2, 1, 3):
        py_copy(level(d), y).start()
    hop(0, 3)
    hop(1, 2)
    gather_y(0)
    gather_y(1)
    for j in (3, 4, 5):
        hop(0, j + 1)
        hop(1, j)
    hop(0, 7)
    hop(1, 6)
    gather_core(0)
    gather_core(1)
    for d in (1, 3, 2):
        py_copy(y, level(d)).wait_recv()
    pf_copy(core).start()
    red[SRC * 72 :] = jnp.zeros((96, 8, 128), F32)
    hop(0, 8)
    choose(0)
    hop(1, 7)
    hop(1, 8)
    choose(1)
    pf_copy(1 - core).wait_recv()

    pick = lax.broadcasted_iota(jnp.int32, (ROWS, NV), 0) + own == lax.broadcasted_iota(jnp.int32, (ROWS, NV), 1)
    pick = jnp.where(pick, F32(1), F32(0)).astype(BF16)
    for s in range(SRC):
        for a in range(2):
            block = pg[:, :, s, a].reshape(NV, NV)
            pct[a * 64 + s * ROWS : a * 64 + (s + 1) * ROWS] = nt(pick, block).astype(BF16)

    def left_side(b):
        fw_copy(b, 1 - core).wait_recv()

        @pl.loop(3 * b, 3 * b + 3)
        def _(a):
            u = nt(pct[...], et[a, :, :NV])
            v = nt(pct[...], et[a, :, NV:])
            lt[a, 0] = (u[:64] - v[64:]).reshape(SRC, ROWS, NV)
            lt[a, 1] = (v[:64] + u[64:]).reshape(SRC, ROWS, NV)

    def traces(b):
        @pl.loop(0, SRC)
        def _(s):
            xh_copy(b, s).wait_recv()
            here = jnp.full((3, ROWS, 2 * NV), src[s] // ring, jnp.int32) == xh
            block = jnp.where(here, sel[b, s].astype(F32), come[b, s].astype(F32))
            block = block.astype(BF16).reshape(3 * ROWS, 2 * NV)
            both = jnp.concatenate([block[:, :NV], block[:, NV:]], axis=0)
            u = nt(both, pg[:, :, s, 0].reshape(NV, NV))
            v = nt(both, pg[:, :, s, 1].reshape(NV, NV))
            wb[0] = (u[: 3 * ROWS] + v[3 * ROWS :]).reshape(3, ROWS, NV)
            wb[1] = (u[3 * ROWS :] - v[: 3 * ROWS]).reshape(3, ROWS, NV)

            @pl.loop(0, OPS)
            def _(a):
                l_re = lt[a, 0, s]
                l_im = lt[a, 1, s]
                for q in range(3):
                    w_re = wb[0, q]
                    w_im = wb[1, q]
                    at = s * 72 + a * OPS + 3 * b + q
                    red[at] = fold(l_re * w_re - l_im * w_im)
                    red[at + 36] = fold(l_re * w_im + l_im * w_re)

    left_side(0)
    left_side(1)
    traces(0)
    traces(1)

    sums = jnp.sum(red[...], axis=1)
    res[r] = nt(jnp.ones((8, 128), F32), sums, lax.Precision.HIGHEST)[:1]

    @pl.loop(1, space)
    def _(d):
        ps_copy((r + d) % space, r).start()

    lane = lax.broadcasted_iota(jnp.int32, (64, 384), 1)
    line = lax.broadcasted_iota(jnp.int32, (64, 384), 0)
    sink = jnp.full((64, 384), -1, jnp.int32)
    for o in range(OPS):
        sink = jnp.where((line & 7) == o, pos[o], sink)
    rows_taken = jnp.where((lane // 36 == line // 8) & ((lane % 36) // 6 == sink), F32(1), F32(0))
    lane = lax.broadcasted_iota(jnp.int32, (384, 128), 1)
    line = lax.broadcasted_iota(jnp.int32, (384, 128), 0)
    source = jnp.full((384, 128), -1, jnp.int32)
    for o in range(OPS):
        source = jnp.where(lane == o, pos[o], source)
    columns_taken = jnp.where(line % 6 == source, F32(1), F32(0))
    equal = lax.broadcasted_iota(jnp.int32, (64, 128), 1) == (lax.broadcasted_iota(jnp.int32, (64, 128), 0) & 7)

    @pl.loop(1, space)
    def _(d):
        ps_copy(r, (r + d) % space).wait_recv()

    total = res[0]
    for q in range(1, space):
        total = total + res[q]
    matrix = lax.dot_general(
        rows_taken * total, columns_taken, (((1,), (0,)), ((), ())),
        precision=lax.Precision.HIGHEST, preferred_element_type=F32,
    )
    diagonal = jnp.where(equal, matrix, F32(0))
    down = jnp.sum(diagonal, axis=1, keepdims=True).reshape(SRC, 2, 8, 1)
    over = jnp.sum(diagonal.reshape(SRC, 2, 8, 128), axis=2, keepdims=True)
    matrix = matrix.reshape(SRC, 2, 8, 128)
    pair = (
        down[:, 0] * over[:, 0] - down[:, 1] * over[:, 1],
        down[:, 0] * over[:, 1] + down[:, 1] * over[:, 0],
    )
    for c in range(2):
        for a in range(OPS):
            corr_ref[:, a, c] = matrix[:, c, a, :OPS]
            two_ref[:, a, c] = pair[c][:, a, :OPS]

    for p in range(6):
        z_copy(p).wait_send()

    @pl.when(relays)
    def _():
        for n in range(2):
            zr_copy(n).wait_send()


    def drain(ref, send):
        remote(ref, ref, send, pf_recv, "space", partner).wait_send()

    @pl.loop(0, OPS)
    def _(i):
        pair_copy(i).wait_send()
        drain(sb.at[i, pl.ds(0, 3)], rs_send.at[i])
        xs_copy(i).wait_send()

    for b in range(2):
        gx_copy(b, own_rows()).wait_send()
        drain(et.at[three(b), pl.ds(0, 96)], gy_send.at[b])
        fw_copy(b, core).wait_send()
        drain(sel.at[b], xh_send.at[b])
        for w in range(2):
            for k in range(1, hops[w] + 1):
                hop_copy(b, w, k).wait_send()

    px_copy(x).wait_send()
    drain(pg.at[pl.ds(0, 6), 0], py_send)
    pf_copy(core).wait_send()
    drain(res.at[pl.ds(0, 15)], ps_send)


def fused(ring, v, momenta, displacement, sources, p):
    dma = pltpu.SemaphoreType.DMA
    most = ring // 2 + 1
    return pl.pallas_call(
        functools.partial(kernel, ring),
        out_shape=[jax.ShapeDtypeStruct((SRC, OPS, 2, OPS), F32)] * 2,
        in_specs=[
            pl.BlockSpec(memory_space=pl.ANY),
            pl.BlockSpec(memory_space=pl.ANY),
            pl.BlockSpec(memory_space=pl.ANY),
            pl.BlockSpec(memory_space=pl.ANY),
            pl.BlockSpec(memory_space=pl.ANY),
        ],
        out_specs=[pl.BlockSpec(memory_space=pltpu.VMEM)] * 2,
        scratch_shapes=[
            pltpu.VMEM((3, 6, NV, NV), BF16),
            pltpu.VMEM((6, NV, NV), BF16),
            pltpu.VMEM((2, NV, NV), BF16),
            pltpu.VMEM((NV, 6 * NV), BF16),
            pltpu.VMEM((6 * NV, 2 * NV), BF16),
            pltpu.VMEM((OPS, 2, NV, 128), F32),
            pltpu.VMEM((OPS, NV, 2 * NV), F32),
            pltpu.VMEM((OPS, 128, 2 * NV), F32),
            pltpu.VMEM((OPS, 4, 2 * ROWS, 2 * NV), BF16),
            pltpu.VMEM((OPS, 4, 2 * ROWS, 2 * NV), BF16),
            pltpu.VMEM((OPS, 2, ROWS, 2 * NV), F32),
            pltpu.VMEM((OPS, ROWS, 2 * NV), F32),
            pltpu.VMEM((OPS, NV, 2 * NV), BF16),
            pltpu.VMEM((ring, 3, ROWS, 2 * NV), BF16),
            pltpu.VMEM((ring, 3, ROWS, 2 * NV), BF16),
            pltpu.VMEM((2, SRC, 3, ROWS, 2 * NV), BF16),
            pltpu.VMEM((2, SRC, 3, ROWS, 2 * NV), BF16),
            pltpu.VMEM((CHIPS, 2, SRC, 2, ROWS, NV), BF16),
            pltpu.VMEM((128, NV), BF16),
            pltpu.VMEM((OPS, 2, SRC, ROWS, NV), F32),
            pltpu.VMEM((2, 3, ROWS, NV), F32),
            pltpu.VMEM((384, 8, 128), F32),
            pltpu.VMEM((2 * CHIPS, 1, 384), F32),
            pltpu.SMEM((3, OPS), jnp.int32),
            pltpu.SMEM((OPS,), jnp.int32),
            pltpu.SMEM((SRC,), jnp.int32),
            pltpu.SMEM((OPS,), jnp.int32),
            pltpu.SMEM((OPS,), jnp.int32),
            pltpu.SMEM((OPS,), jnp.int32),
            dma((5,)),
            dma((6,)), dma((6,)),
            dma((2,)), dma((2,)),
            dma((OPS,)), dma((OPS,)),
            dma((OPS,)), dma((OPS, 4)),
            dma((OPS,)), dma((OPS,)),
            dma((2,)), dma((2,)),
            dma((2,)), dma((2, 4)),
            dma((2,)), dma((2,)),
            dma((2,)), dma((2, SRC)),
            dma((2, 2, most)), dma((2, 2, most)),
            dma, dma,
            dma, dma((4,)),
            dma, dma,
            dma, dma((2 * CHIPS,)),
        ],
        compiler_params=pltpu.CompilerParams(
            collective_id=0, has_side_effects=True
        ),
    )(v, momenta, displacement, sources, p)


def body(eigenvectors, momenta, displacement, source_times, perambulators):
    ring = lax.axis_size("tm") // 2
    outputs = fused(
        ring,
        eigenvectors.reshape(6, NV, NV),
        momenta.T,
        displacement,
        source_times,
        perambulators.reshape(SRC, 2, ROWS, NV),
    )
    return tuple(jnp.transpose(out, (0, 2, 1, 3))[None] for out in outputs)


def solution(mesh):
    placed = (
        P("tm", None, None, "space", None, None),
        P(),
        P(),
        P(),
        P("tm", None, None, "space", None),
    )
    return jax.shard_map(
        body,
        mesh=mesh,
        in_specs=placed,
        out_specs=(P("tm", None, None, None, None), P("tm", None, None, None, None)),
        check_vma=False,
    )
```

```python
import functools
import math

import jax
import jax.numpy as jnp
from jax import lax
from jax.experimental import pallas as pl
from jax.experimental.pallas import tpu as pltpu
from jax.sharding import PartitionSpec as P

MESH = pl.DeviceIdType.MESH
F32 = jnp.float32
BF16 = jnp.bfloat16
OPS = 6
SRC = 4
CHIPS = 8
NV = 256
ROWS = 16
COSINE = [math.cos(2.0 * math.pi * m / 16) for m in range(16)]
SINE = [math.sin(2.0 * math.pi * m / 16) for m in range(16)]


def nt(left, right, precision=None):
    return lax.dot_general(
        left, right, (((1,), (1,)), ((), ())), precision=precision, preferred_element_type=F32
    )


def fold(block):
    halves = block[:, :128] + block[:, 128:]
    return halves[:8] + halves[8:]


def kernel(
    ring, v_hbm, mom_hbm, disp_hbm, src_hbm, p_hbm, out_ref,
    sh3, zb, zr, vt, rhs, ctb, part, prt, sb, rsr, xs, xr, et, ga, gb, sel, come, pg, pct, lt, wb, red, res,
    mom, disp, src, perm, pos, dsort,
    loc_sem, zs_send, zs_recv, zr_send, zr_recv, pr_send, pr_recv, rs_send, rs_recv, xs_send, xs_recv,
    gx_send, gx_recv, gy_send, gy_recv, fw_send, fw_recv, xh_send, xh_recv, hop_send, hop_recv,
    px_send, px_recv, py_send, py_recv, pf_send, pf_recv, ps_send, ps_recv,
):
    space = 2 * CHIPS
    half = ring // 2
    hops = (half, ring - 1 - half)
    rings = (ga, gb)
    r = lax.axis_index("space")
    t = lax.axis_index("tm")
    chip = r // 2
    core = r % 2
    xh = t // ring
    z = t % ring
    partner = 2 * chip + 1 - core
    ahead = (xh * ring + (z + 1) % ring, xh * ring + (z + ring - 1) % ring)
    across = (1 - xh) * ring + z
    own = core * 128 + chip * ROWS

    y = chip // 2
    x = chip % 2
    beside = 2 * (2 * y + 1 - x) + core

    def level(d):
        return (y + d) % 4

    def on_level(q):
        return 2 * (2 * q + x) + core

    def remote(src_ref, dst_ref, send, recv, axis, index):
        return pltpu.make_async_remote_copy(
            src_ref=src_ref, dst_ref=dst_ref, send_sem=send, recv_sem=recv,
            device_id={axis: index}, device_id_type=MESH,
        )

    def rows_of(q):
        return pl.ds(pl.multiple_of(core * 128 + q * 2 * ROWS, 2 * ROWS), 2 * ROWS)

    def own_rows():
        return pl.ds(pl.multiple_of(own, ROWS), ROWS)

    def beside_rows():
        return pl.ds(pl.multiple_of(core * 128 + y * 2 * ROWS + (1 - x) * ROWS, ROWS), ROWS)

    def three(b):
        return pl.ds(3 * b, 3)

    def side(c):
        return pl.ds(pl.multiple_of(c * 128, 128), 128)

    def z_copy(p):
        return remote(sh3.at[0, p], zb.at[p], zs_send.at[p], zs_recv.at[p], "space", (r + space - 1) % space)

    relays = (x == 0) & (core == 0)

    def zr_copy(n):
        return remote(sh3.at[0, 2 + 3 * n], zr.at[n], zr_send.at[n], zr_recv.at[n], "space", (r + space - 4) % space)

    def pass_on(n):
        return remote(zr.at[n], zb.at[2 + 3 * n], zs_send.at[2 + 3 * n], zs_recv.at[2 + 3 * n], "space", (r + 3) % space)

    def pair_copy(i):
        return remote(part.at[i, side(1 - core)], prt.at[i], pr_send.at[i], pr_recv.at[i], "space", partner)

    def rs_copy(i, to, frm):
        return remote(sb.at[i, to], rsr.at[i, frm], rs_send.at[i], rs_recv.at[i, frm], "space", on_level(to))

    def xs_copy(i):
        return remote(xs.at[i, 1 - x], xr.at[i], xs_send.at[i], xs_recv.at[i], "space", beside)

    def gx_copy(b, rows):
        part_of = et.at[three(b), rows]
        return remote(part_of, part_of, gx_send.at[b], gx_recv.at[b], "space", beside)

    def gy_copy(b, to, frm):
        part_of = et.at[three(b), rows_of(frm)]
        return remote(part_of, part_of, gy_send.at[b], gy_recv.at[b, frm], "space", on_level(to))

    def fw_copy(b, c):
        part_of = et.at[three(b), side(c)]
        return remote(part_of, part_of, fw_send.at[b], fw_recv.at[b], "space", partner)

    def xh_copy(b, s):
        return remote(sel.at[b, s], come.at[b, s], xh_send.at[b], xh_recv.at[b, s], "tm", across)

    def hop_copy(b, w, j):
        origin = (z + ring - j + 1) % ring if w == 0 else (z + j - 1) % ring
        slot = rings[b].at[origin]
        return remote(slot, slot, hop_send.at[b, w, j], hop_recv.at[b, w, j], "tm", ahead[w])

    def hop_done(b, w, j):
        origin = (z + ring - j) % ring if w == 0 else (z + j) % ring
        slot = rings[b].at[origin]
        remote(slot, slot, hop_send.at[b, w, j], hop_recv.at[b, w, j], "tm", ahead[w]).wait_recv()

    def px_copy(to):
        return remote(p_hbm, pg.at[2 * y + to, core], px_send, px_recv, "space", beside)

    def py_copy(to, frm):
        part_of = pg.at[pl.ds(2 * frm, 2), core]
        return remote(part_of, part_of, py_send, py_recv.at[frm], "space", on_level(to))

    def pf_copy(c):
        return remote(pg.at[:, c], pg.at[:, c], pf_send, pf_recv, "space", partner)

    def ps_copy(to, frm):
        return remote(res.at[frm], res.at[frm], ps_send, ps_recv.at[frm], "space", to)

    barrier = pltpu.get_barrier_semaphore()
    v_copy = pltpu.make_async_copy(v_hbm, sh3.at[0], loc_sem.at[0])
    v_copy.start()
    p_copy = pltpu.make_async_copy(p_hbm, pg.at[chip, core], loc_sem.at[1])
    p_copy.start()
    small = [
        pltpu.make_async_copy(a, b, loc_sem.at[n])
        for n, (a, b) in enumerate(((mom_hbm, mom), (disp_hbm, disp), (src_hbm, src)), 2)
    ]
    for copy in small:
        copy.start()

    @pl.loop(1, space)
    def _(d):
        pl.semaphore_signal(barrier, inc=1, device_id={"space": (r + d) % space}, device_id_type=MESH)

    for other in (*ahead, across):
        pl.semaphore_signal(barrier, inc=1, device_id={"tm": other}, device_id_type=MESH)

    v_copy.wait()
    pl.semaphore_wait(barrier, space + 2)

    @pl.when(relays)
    def _():
        for n in range(2):
            zr_copy(n).start()

    for color in range(2):
        z_copy(color).start()
        z_copy(3 + color).start()

    @pl.when(jnp.logical_not(relays))
    def _():
        z_copy(2).start()
        z_copy(5).start()

    for copy in small:
        copy.wait()
    place = []
    for o in range(OPS):
        before = jnp.int32(0)
        for q in range(OPS):
            if q != o:
                low = disp[q] <= disp[o] if q < o else disp[q] < disp[o]
                before = before + jnp.where(low, 1, 0)
        place.append(before)
        pos[o] = before
    for j in range(OPS):
        which = jnp.int32(0)
        for o in range(OPS):
            which = which + jnp.where(place[o] == j, o, 0)
        perm[j] = which
        dsort[j] = disp[which]

    site = lax.broadcasted_iota(jnp.int32, (128, NV), 1)
    line = lax.broadcasted_iota(jnp.int32, (128, NV), 0)
    turns = jnp.zeros((128, NV), jnp.int32)
    for j in range(OPS):
        o = perm[j]
        turns = jnp.where(line == j, mom[0, o] * (site & 15) + mom[1, o] * (site >> 4) + mom[2, o] * r, turns)
    turns = turns & 15
    for a, table in enumerate((COSINE, SINE)):
        values = jnp.zeros((128, NV), F32)
        for m in range(16):
            values = jnp.where(turns == m, F32(table[m]), values)
        flipped = values.T
        for j in range(OPS):
            ctb[j, a] = jnp.broadcast_to(flipped[:, j : j + 1], (NV, 128))

    row = lax.broadcasted_iota(jnp.int32, (NV, NV), 0)
    wraps = (row & 15) == 15
    for p in range(6):
        wide = sh3[0, p].astype(F32)
        vt[:, p * NV : (p + 1) * NV] = wide.T.astype(BF16)
        sh3[1, p] = jnp.where(wraps, pltpu.roll(wide, 15, 0), pltpu.roll(wide, NV - 1, 0)).astype(BF16)
        sh3[2, p, : NV - 16] = sh3[0, p, 16:]
        sh3[2, p, NV - 16 :] = sh3[0, p, :16]

    def weigh(i, color, beyond):
        d = dsort[i]
        kept = jnp.minimum(d, 2)

        @pl.loop(0, 4)
        def _(part_of):
            top = pl.multiple_of(part_of * 64, 64)
            rows = pl.ds(top, 64)
            re = sh3[kept, color, rows].astype(F32)
            im = sh3[kept, 3 + color, rows].astype(F32)
            if beyond:
                moved = jnp.full((64, NV), d, jnp.int32) == 3
                re = jnp.where(moved, zb[color, rows].astype(F32), re)
                im = jnp.where(moved, zb[3 + color, rows].astype(F32), im)
            cosine = ctb[i, 0, rows]
            sine = ctb[i, 1, rows]
            cosine = jnp.concatenate([cosine, cosine], axis=1)
            sine = jnp.concatenate([sine, sine], axis=1)
            w_re = (cosine * re + sine * im).astype(BF16)
            w_im = (cosine * im - sine * re).astype(BF16)
            upper = pl.ds(pl.multiple_of(color * NV + top, 64), 64)
            lower = pl.ds(pl.multiple_of((3 + color) * NV + top, 64), 64)
            rhs[upper, :NV] = w_re
            rhs[upper, NV:] = w_im
            rhs[lower, :NV] = w_im
            rhs[lower, NV:] = -w_re

    def color_sum(color):
        return sum(
            jnp.dot(
                vt[:, p * NV : (p + 1) * NV], rhs[p * NV : (p + 1) * NV], preferred_element_type=F32
            )
            for p in (color, 3 + color)
        )

    def over_y(i):
        pair_copy(i).wait_recv()
        sb[i] = (part[i, side(core)] + prt[i]).astype(BF16).reshape(4, 2 * ROWS, 2 * NV)
        for d in (2, 1, 3):
            rs_copy(i, level(d), y).start()

    def over_x(i):
        ours = pl.ds(pl.multiple_of(y * 2 * ROWS, 2 * ROWS), 2 * ROWS)
        total = part[i, rows_of(y)] + prt[i, ours]
        for d in (1, 3, 2):
            rs_copy(i, y, level(d)).wait_recv()
            total = total + rsr[i, level(d)].astype(F32)
        xs[i] = total.reshape(2, ROWS, 2 * NV)
        xs_copy(i).start()

    def finish(i, b):
        xs_copy(i).wait_recv()
        value = (xs[i, x] + xr[i]).astype(BF16)
        et[i, own_rows()] = value
        rings[b][z, i - 3 * b] = value

    def near_batch():
        @pl.loop(0, 3)
        def _(i):
            @pl.loop(0, 3)
            def _(color):
                weigh(i, color, False)

            part[i] = jnp.dot(vt[...], rhs[...], preferred_element_type=F32)
            pair_copy(i).start()

    def far_batch(color):
        z_copy(color).wait_recv()
        z_copy(3 + color).wait_recv()

        @pl.loop(3, OPS)
        def _(i):
            weigh(i, color, True)
            if color == 0:
                part[i] = color_sum(color)
            else:
                part[i] += color_sum(color)
            if color == 2:
                pair_copy(i).start()

    def each(stage, first):
        @pl.loop(first, first + 3)
        def _(i):
            stage(i)

    def start_ring(b):
        for w in range(2):
            hop_copy(b, w, 1).start()

    def hop(b, j):
        for w in range(2):
            if j <= hops[w]:
                hop_done(b, w, j)
                if j < hops[w]:
                    hop_copy(b, w, j + 1).start()

    def choose(b):
        @pl.loop(0, SRC)
        def _(s):
            sel[b, s] = rings[b][src[s] & (ring - 1)]
            xh_copy(b, s).start()

    def gather_y(b):
        gx_copy(b, beside_rows()).wait_recv()
        for d in (2, 1, 3):
            gy_copy(b, level(d), y).start()

    def gather_core(b):
        for d in (1, 3, 2):
            gy_copy(b, y, level(d)).wait_recv()
        fw_copy(b, core).start()

    near_batch()

    @pl.when(relays)
    def _():
        for n in range(2):
            zr_copy(n).wait_recv()
            pass_on(n).start()

    far_batch(0)
    each(over_y, 0)
    far_batch(1)
    far_batch(2)

    @pl.when(core == 0)
    def _():
        each(over_x, 0)

    each(over_y, 3)

    @pl.when(core == 1)
    def _():
        each(over_x, 0)

    each(lambda i: finish(i, 0), 0)
    start_ring(0)
    each(over_x, 3)
    hop(0, 1)
    each(lambda i: finish(i, 1), 3)
    start_ring(1)
    gx_copy(0, own_rows()).start()
    gx_copy(1, own_rows()).start()
    px_copy(x).start()
    hop(0, 2)
    hop(1, 1)
    p_copy.wait()
    px_copy(1 - x).wait_recv()
    for d in (2, 1, 3):
        py_copy(level(d), y).start()
    hop(0, 3)
    hop(1, 2)
    gather_y(0)
    gather_y(1)
    for j in (3, 4):
        hop(0, j + 1)
        hop(1, j)
    for d in (1, 3, 2):
        py_copy(y, level(d)).wait_recv()
    pf_copy(core).start()
    hop(0, 6)
    hop(1, 5)
    gather_core(0)
    gather_core(1)
    hop(0, 7)
    hop(1, 6)
    red[SRC * 72 :] = jnp.zeros((96, 8, 128), F32)
    hop(0, 8)
    choose(0)
    hop(1, 7)
    pf_copy(1 - core).wait_recv()

    pick = lax.broadcasted_iota(jnp.int32, (ROWS, NV), 0) + own == lax.broadcasted_iota(jnp.int32, (ROWS, NV), 1)
    pick = jnp.where(pick, F32(1), F32(0)).astype(BF16)
    for s in range(SRC):
        for a in range(2):
            block = pg[:, :, s, a].reshape(NV, NV)
            pct[a * 64 + s * ROWS : a * 64 + (s + 1) * ROWS] = nt(pick, block).astype(BF16)

    def left_side(b):
        fw_copy(b, 1 - core).wait_recv()

        @pl.loop(3 * b, 3 * b + 3)
        def _(a):
            u = nt(pct[...], et[a, :, :NV])
            v = nt(pct[...], et[a, :, NV:])
            lt[a, 0] = (u[:64] - v[64:]).reshape(SRC, ROWS, NV)
            lt[a, 1] = (v[:64] + u[64:]).reshape(SRC, ROWS, NV)

    def traces(b):
        @pl.loop(0, SRC)
        def _(s):
            xh_copy(b, s).wait_recv()
            here = jnp.full((3, ROWS, 2 * NV), src[s] // ring, jnp.int32) == xh
            block = jnp.where(here, sel[b, s].astype(F32), come[b, s].astype(F32))
            block = block.astype(BF16).reshape(3 * ROWS, 2 * NV)
            both = jnp.concatenate([block[:, :NV], block[:, NV:]], axis=0)
            u = nt(both, pg[:, :, s, 0].reshape(NV, NV))
            v = nt(both, pg[:, :, s, 1].reshape(NV, NV))
            wb[0] = (u[: 3 * ROWS] + v[3 * ROWS :]).reshape(3, ROWS, NV)
            wb[1] = (u[3 * ROWS :] - v[: 3 * ROWS]).reshape(3, ROWS, NV)

            @pl.loop(0, OPS)
            def _(a):
                l_re = lt[a, 0, s]
                l_im = lt[a, 1, s]
                for q in range(3):
                    w_re = wb[0, q]
                    w_im = wb[1, q]
                    at = s * 72 + a * OPS + 3 * b + q
                    red[at] = fold(l_re * w_re - l_im * w_im)
                    red[at + 36] = fold(l_re * w_im + l_im * w_re)

    left_side(0)
    left_side(1)
    hop(1, 8)
    choose(1)
    traces(0)
    traces(1)

    sums = jnp.sum(red[...], axis=1)
    res[r] = nt(jnp.ones((8, 128), F32), sums, lax.Precision.HIGHEST)[:1]

    @pl.loop(1, space)
    def _(d):
        ps_copy((r + d) % space, r).start()

    lane = lax.broadcasted_iota(jnp.int32, (64, 384), 1)
    line = lax.broadcasted_iota(jnp.int32, (64, 384), 0)
    sink = jnp.full((64, 384), -1, jnp.int32)
    for o in range(OPS):
        sink = jnp.where((line & 7) == o, pos[o], sink)
    rows_taken = jnp.where((lane // 36 == line // 8) & ((lane % 36) // 6 == sink), F32(1), F32(0))
    lane = lax.broadcasted_iota(jnp.int32, (384, 128), 1)
    line = lax.broadcasted_iota(jnp.int32, (384, 128), 0)
    source = jnp.full((384, 128), -1, jnp.int32)
    for o in range(OPS):
        source = jnp.where(lane == o, pos[o], source)
    columns_taken = jnp.where(line % 6 == source, F32(1), F32(0))
    equal = lax.broadcasted_iota(jnp.int32, (64, 128), 1) == (lax.broadcasted_iota(jnp.int32, (64, 128), 0) & 7)

    @pl.loop(1, space)
    def _(d):
        ps_copy(r, (r + d) % space).wait_recv()

    total = res[0]
    for q in range(1, space):
        total = total + res[q]
    matrix = lax.dot_general(
        rows_taken * total, columns_taken, (((1,), (0,)), ((), ())),
        precision=lax.Precision.HIGHEST, preferred_element_type=F32,
    )
    diagonal = jnp.where(equal, matrix, F32(0))
    down = jnp.sum(diagonal, axis=1, keepdims=True).reshape(SRC, 2, 8, 1)
    over = jnp.sum(diagonal.reshape(SRC, 2, 8, 128), axis=2, keepdims=True)
    matrix = matrix.reshape(SRC, 2, 8, 128)
    pair = (
        down[:, 0] * over[:, 0] - down[:, 1] * over[:, 1],
        down[:, 0] * over[:, 1] + down[:, 1] * over[:, 0],
    )
    for c in range(2):
        for a in range(OPS):
            out_ref[0, :, a, c] = matrix[:, c, a, :OPS]
            out_ref[1, :, a, c] = pair[c][:, a, :OPS]

    for p in range(6):
        z_copy(p).wait_send()

    @pl.when(relays)
    def _():
        for n in range(2):
            zr_copy(n).wait_send()


    def drain(ref, send):
        remote(ref, ref, send, pf_recv, "space", partner).wait_send()

    @pl.loop(0, OPS)
    def _(i):
        pair_copy(i).wait_send()
        drain(sb.at[i, pl.ds(0, 3)], rs_send.at[i])
        xs_copy(i).wait_send()

    for b in range(2):
        gx_copy(b, own_rows()).wait_send()
        drain(et.at[three(b), pl.ds(0, 96)], gy_send.at[b])
        fw_copy(b, core).wait_send()
        drain(sel.at[b], xh_send.at[b])
        for w in range(2):
            for k in range(1, hops[w] + 1):
                hop_copy(b, w, k).wait_send()

    px_copy(x).wait_send()
    drain(pg.at[pl.ds(0, 6), 0], py_send)
    pf_copy(core).wait_send()
    drain(res.at[pl.ds(0, 15)], ps_send)


def fused(ring, v, momenta, displacement, sources, p):
    dma = pltpu.SemaphoreType.DMA
    most = ring // 2 + 1
    return pl.pallas_call(
        functools.partial(kernel, ring),
        out_shape=jax.ShapeDtypeStruct((2, SRC, OPS, 2, OPS), F32),
        in_specs=[
            pl.BlockSpec(memory_space=pl.ANY),
            pl.BlockSpec(memory_space=pl.ANY),
            pl.BlockSpec(memory_space=pl.ANY),
            pl.BlockSpec(memory_space=pl.ANY),
            pl.BlockSpec(memory_space=pl.ANY),
        ],
        out_specs=pl.BlockSpec(memory_space=pltpu.VMEM),
        scratch_shapes=[
            pltpu.VMEM((3, 6, NV, NV), BF16),
            pltpu.VMEM((6, NV, NV), BF16),
            pltpu.VMEM((2, NV, NV), BF16),
            pltpu.VMEM((NV, 6 * NV), BF16),
            pltpu.VMEM((6 * NV, 2 * NV), BF16),
            pltpu.VMEM((OPS, 2, NV, 128), F32),
            pltpu.VMEM((OPS, NV, 2 * NV), F32),
            pltpu.VMEM((OPS, 128, 2 * NV), F32),
            pltpu.VMEM((OPS, 4, 2 * ROWS, 2 * NV), BF16),
            pltpu.VMEM((OPS, 4, 2 * ROWS, 2 * NV), BF16),
            pltpu.VMEM((OPS, 2, ROWS, 2 * NV), F32),
            pltpu.VMEM((OPS, ROWS, 2 * NV), F32),
            pltpu.VMEM((OPS, NV, 2 * NV), BF16),
            pltpu.VMEM((ring, 3, ROWS, 2 * NV), BF16),
            pltpu.VMEM((ring, 3, ROWS, 2 * NV), BF16),
            pltpu.VMEM((2, SRC, 3, ROWS, 2 * NV), BF16),
            pltpu.VMEM((2, SRC, 3, ROWS, 2 * NV), BF16),
            pltpu.VMEM((CHIPS, 2, SRC, 2, ROWS, NV), BF16),
            pltpu.VMEM((128, NV), BF16),
            pltpu.VMEM((OPS, 2, SRC, ROWS, NV), F32),
            pltpu.VMEM((2, 3, ROWS, NV), F32),
            pltpu.VMEM((384, 8, 128), F32),
            pltpu.VMEM((2 * CHIPS, 1, 384), F32),
            pltpu.SMEM((3, OPS), jnp.int32),
            pltpu.SMEM((OPS,), jnp.int32),
            pltpu.SMEM((SRC,), jnp.int32),
            pltpu.SMEM((OPS,), jnp.int32),
            pltpu.SMEM((OPS,), jnp.int32),
            pltpu.SMEM((OPS,), jnp.int32),
            dma((5,)),
            dma((6,)), dma((6,)),
            dma((2,)), dma((2,)),
            dma((OPS,)), dma((OPS,)),
            dma((OPS,)), dma((OPS, 4)),
            dma((OPS,)), dma((OPS,)),
            dma((2,)), dma((2,)),
            dma((2,)), dma((2, 4)),
            dma((2,)), dma((2,)),
            dma((2,)), dma((2, SRC)),
            dma((2, 2, most)), dma((2, 2, most)),
            dma, dma,
            dma, dma((4,)),
            dma, dma,
            dma, dma((2 * CHIPS,)),
        ],
        compiler_params=pltpu.CompilerParams(
            collective_id=0, has_side_effects=True
        ),
    )(v, momenta, displacement, sources, p)


def body(eigenvectors, momenta, displacement, source_times, perambulators):
    ring = lax.axis_size("tm") // 2
    outputs = fused(
        ring,
        eigenvectors.reshape(6, NV, NV),
        momenta.T,
        displacement,
        source_times,
        perambulators.reshape(SRC, 2, ROWS, NV),
    )
    return tuple(jnp.transpose(out, (0, 2, 1, 3))[None] for out in (outputs[0], outputs[1]))


def solution(mesh):
    placed = (
        P("tm", None, None, "space", None, None),
        P(),
        P(),
        P(),
        P("tm", None, None, "space", None),
    )
    return jax.shard_map(
        body,
        mesh=mesh,
        in_specs=placed,
        out_specs=(P("tm", None, None, None, None), P("tm", None, None, None, None)),
        check_vma=False,
    )
```
